32 devices in a mesh: groups: 2 (over y), state: 4 (over z), type: 4 (over x, core).
Axes of the slice: x: 2, y: 2, z: 4, core: 2. Of those that a mesh axis runs over, the one named last changes fastest.
Arguments:
- value_in: bfloat16 [16384, 2048], P(('groups', 'state'), 'type'), parts along dimension 0, may hold values from -7.5 to 7.5
- cotangent: bfloat16 [16384, 2048], P(('groups', 'state'), 'type'), parts along dimension 0, may hold values from -100 to 100
- state_util: float32 [2, 16384], P(None, ('groups', 'state')), parts along dimension 1, may hold values from -300 to 300
- taste: float32 [2, 4096], P(None, ('groups', 'type')), parts along dimension 1, may hold values from -6 to 6
- tiles: bfloat16 [128, 2, 6, 128, 128], P(('groups', 'state')), parts along dimension 0, may hold values from 0 to 0.0051879883
- dest_block: int32 [128, 2, 6], P(('groups', 'state')), parts along dimension 0, may hold values from 0 to 63, as said below
- counts: int32 [128, 2], P(('groups', 'state')), parts along dimension 0, may hold values from 1 to 6
Outputs:
- value_out: float32 [16384, 2048], P(('groups', 'state'), 'type'), parts along dimension 0
- adjoint: float32 [16384, 2048], P(('groups', 'state'), 'type'), parts along dimension 0
- grad_util: float32 [2, 16384], P(None, ('groups', 'state')), parts along dimension 1
- grad_taste: float32 [2, 4096], P(None, ('groups', 'type')), parts along dimension 1
The draws below stay inside these ranges and needn't reach their ends.
There are 2 independent parts, one for each index of `groups`. The reference program is written for one: setup_inputs(seed, part) draws one part's arguments, and reference() takes and returns one part's arrays. A program takes and returns all parts, laid end to end along the dimension named above; each array names one. Nothing has to cross between parts.
Inputs may be any that keep to these rules, and one draw needn't show every extreme that they name: `dest_block`: entries at or beyond a list's count name blocks of the list's own run of 16 blocks. In each run of 16 blocks exactly 16 used entries name blocks outside the run, at most 6 of them in any one other run, and exactly 6 in some other run.
All inputs are finite; a program needn't handle non-finite values.
Results may differ from the reference program's by a relative error of at most 0.0012.
Values may be sent and summed in bfloat16 or wider, within the bound.
A program may use at most 192 MiB of HBM per device.

```python
import math
import jax
import jax.numpy as jnp
from jax import lax

B_DEV = 16
M = 6
TILE = 128
K = 2048
NB = 64
S = 8192
REMOTE = 16
CAP = 6


def integer_lists(key):
    device_count = NB // B_DEV
    entry_total = B_DEV * 2 * M
    list_total = B_DEV * 2
    count_draw = jax.random.randint(jax.random.fold_in(key, 11), (device_count * list_total,), 1, M + 1)
    high_spot = jax.random.randint(jax.random.fold_in(key, 12), (), 0, NB * 2)
    low_spot = (high_spot + 1 + jax.random.randint(jax.random.fold_in(key, 13), (), 0, NB * 2 - 1)) % (NB * 2)
    count_draw = count_draw.at[high_spot].set(M).at[low_spot].set(1)
    count_grid = count_draw.reshape(device_count, list_total)
    entry_pos = jnp.arange(entry_total, dtype=jnp.int32) % M
    list_pos = jnp.arange(entry_total, dtype=jnp.int32) // M
    used = entry_pos[None, :] < count_grid[:, list_pos]
    keys_one = jax.random.split(jax.random.fold_in(key, 14), device_count)
    ranks = jax.vmap(lambda subkey: jax.random.permutation(subkey, entry_total))(keys_one)
    score = ranks + entry_total * (1 - used.astype(jnp.int32))
    chosen = jnp.argsort(score, axis=1, stable=True)[:, :REMOTE]
    pair_total = (device_count - 1) * CAP
    hot_offset = jax.random.randint(jax.random.fold_in(key, 15), (device_count, 1), 1, device_count)
    keys_two = jax.random.split(jax.random.fold_in(key, 16), device_count)
    pair_rank = jax.vmap(lambda subkey: jax.random.permutation(subkey, pair_total))(keys_two)
    offset_of = 1 + jnp.arange(pair_total, dtype=jnp.int32) // CAP
    priority = pair_rank + pair_total * (offset_of[None, :] != hot_offset).astype(jnp.int32)
    pair_pick = jnp.argsort(priority, axis=1, stable=True)[:, :REMOTE]
    device_ids = jnp.arange(device_count, dtype=jnp.int32)[:, None]
    far_owner = (device_ids + 1 + pair_pick // CAP) % device_count
    owners = jnp.broadcast_to(device_ids, (device_count, entry_total))
    rows = jnp.broadcast_to(device_ids, (device_count, REMOTE))
    owners = owners.at[rows, chosen].set(far_owner)
    inner = jax.random.randint(jax.random.fold_in(key, 17), (device_count, entry_total), 0, B_DEV)
    dest = (owners * B_DEV + inner).reshape(NB, 2, M)
    return (dest.astype(jnp.int32), count_grid.reshape(NB, 2).astype(jnp.int32))


def draw_dest_block(key, part):
    return integer_lists(key)[0]


def draw_counts(key, part):
    return integer_lists(key)[1]


def draw_value_in(key, part):
    noise = jnp.clip(jax.random.normal(jax.random.fold_in(key, 1), (S, K), jnp.float32), -6.0, 6.0)
    offset = jax.random.uniform(jax.random.fold_in(key, 2), (NB, 1, 1), jnp.float32, -1.5, 1.5)
    value = (noise.reshape(NB, TILE, K) + offset).reshape(S, K)
    return value.astype(jnp.bfloat16)


def draw_cotangent(key, part):
    offset = jax.random.uniform(jax.random.fold_in(key, 2), (NB, 1, 1), jnp.float32, -1.5, 1.5)
    noise = jnp.clip(jax.random.normal(jax.random.fold_in(key, 1), (S, K), jnp.float32), -6.0, 6.0)
    base = (noise.reshape(NB, TILE, K) + offset).reshape(S, K)
    row_scale = jnp.exp(jax.random.uniform(jax.random.fold_in(key, 4), (S, 1), jnp.float32, 0.0, math.log(10.0)))
    col_scale = jnp.exp(jax.random.uniform(jax.random.fold_in(key, 5), (1, K), jnp.float32, 0.0, math.log(10.0)))
    return (0.1 * base * row_scale * col_scale).astype(jnp.bfloat16)


def draw_state_util(key, part):
    return jnp.clip(jax.random.normal(jax.random.fold_in(key, 1), (2, S), jnp.float32), -6.0, 6.0)


def shard_levels(stream_key, extent, pieces, low, high):
    factor_of = 1.0
    for position, parts in pieces:
        steps = jax.random.uniform(jax.random.fold_in(jax.random.fold_in(stream_key, 6), position), (parts,), jnp.float32, low / len(pieces), high / len(pieces))
        factor_of = factor_of * jnp.repeat(jnp.exp(steps), extent[position] // parts).reshape((-1,) + (1,) * (len(extent) - 1 - position))
    return factor_of


def bell_draw(rng, shape, width, reach, cuts=(), kind=jnp.bfloat16):
    array = jax.random.normal(rng, shape, jnp.float32) * width
    if len(cuts) > 0:
        array = shard_levels(rng, shape, cuts, -0.22, 0.18) * array
    return jnp.clip(array, min=-reach, max=reach).astype(kind)


def setup_inputs(seed: int = 0, part: int = 0) -> dict:
    arg_keys = jax.random.split(jax.random.key(seed), 8)
    part_splits = jax.random.split(jax.random.fold_in(arg_keys[7], part), 8)
    return {
        "value_in": draw_value_in(jax.random.fold_in(jax.random.fold_in(arg_keys[7], part), 71), part),
        "cotangent": draw_cotangent(jax.random.fold_in(jax.random.fold_in(arg_keys[7], part), 71), part),
        "state_util": draw_state_util(jax.random.fold_in(jax.random.fold_in(arg_keys[7], part), 71), part),
        "taste": bell_draw(part_splits[3], (2, K), 1.0, 6.0, ((1, 4),), jnp.float32),
        "tiles": jnp.clip(0.0051879883 * jax.random.uniform(part_splits[4], (NB, 2, M, TILE, TILE), jnp.float32) ** shard_levels(part_splits[4], (NB, 2, M, TILE, TILE), ((0, 4),), -0.2, 0.2), 0.0, 0.0051879883).astype(jnp.bfloat16),
        "dest_block": draw_dest_block(jax.random.fold_in(jax.random.fold_in(arg_keys[7], part), 71), part),
        "counts": draw_counts(jax.random.fold_in(jax.random.fold_in(arg_keys[7], part), 71), part),
    }


def reference(value_in, cotangent, state_util, taste, tiles, dest_block, counts):
    block_count = tiles.shape[0]
    entry_count = tiles.shape[2]
    tile_rows = tiles.shape[3]
    type_width = value_in.shape[1]
    state_count = value_in.shape[0]
    value_blocks = value_in.reshape(block_count, tile_rows, type_width)
    cot_blocks = cotangent.reshape(block_count, tile_rows, type_width)
    util_blocks = state_util.reshape(2, block_count, tile_rows)

    def sweep(carry, block):
        adjoint, taste_total = carry
        tile_here = tiles[block].astype(jnp.float32)
        dest_here = dest_block[block]
        used = jnp.arange(entry_count, dtype=jnp.int32)[None, :] < counts[block][:, None]
        picked = value_blocks[dest_here].astype(jnp.float32) * used[:, :, None, None].astype(jnp.float32)
        cont = jnp.einsum("amij,amjk->aik", tile_here, picked)
        util_here = lax.dynamic_index_in_dim(util_blocks, block, 1, keepdims=False)
        scores = util_here[:, :, None] + taste[:, None, :] + 0.95 * cont
        largest = jnp.max(scores, axis=0)
        value = largest + jnp.log(jnp.sum(jnp.exp(scores - largest[None]), axis=0))
        prob = jnp.exp(scores - value[None])
        grad_q = cot_blocks[block].astype(jnp.float32)[None] * prob
        grad_u = jnp.sum(grad_q, axis=2) / type_width
        scaled = lax.optimization_barrier((0.95 * grad_q).astype(jnp.bfloat16)).astype(jnp.float32)
        contrib = jnp.einsum("amij,aik->amjk", tile_here, scaled)
        contrib = contrib * used[:, :, None, None].astype(jnp.float32)
        remote = (dest_here // B_DEV) != (block // B_DEV)
        rounded = lax.optimization_barrier(contrib.astype(jnp.bfloat16)).astype(jnp.float32)
        contrib = jnp.where(remote[:, :, None, None], rounded, contrib)
        adjoint = adjoint.at[dest_here.reshape(-1)].add(contrib.reshape(-1, tile_rows, type_width))
        taste_total = taste_total + jnp.sum(grad_q, axis=1)
        return (adjoint, taste_total), (value, grad_u)

    start = (jnp.zeros((block_count, tile_rows, type_width), jnp.float32), jnp.zeros((2, type_width), jnp.float32))
    (adjoint, taste_total), (values, grad_units) = lax.scan(sweep, start, jnp.arange(block_count, dtype=jnp.int32))
    value_out = values.reshape(state_count, type_width)
    grad_util = grad_units.transpose(1, 0, 2).reshape(2, state_count)
    grad_taste = taste_total / state_count
    return value_out, adjoint.reshape(state_count, type_width), grad_util, grad_taste
```

```python
import functools

import jax
import jax.numpy as jnp
from jax import lax
from jax.experimental import pallas as pl
from jax.experimental.pallas import tpu as pltpu
from jax.sharding import PartitionSpec as P

VMEM = pltpu.VMEM
SMEM = pltpu.SMEM
MESH = pl.DeviceIdType.MESH


def smem():
    return pl.BlockSpec(memory_space=SMEM)


def whole(shape):
    return pl.BlockSpec(shape, lambda *g: (0,) * len(shape))


def plan_kernel(dims, me_ref, dest_ref, count_ref, req_ref, look_ref, start_ref, act_ref, pos_ref, slot_ref, fill):
    B, A, M, D, cap = dims
    me = me_ref[0]

    def clear(p, carry):
        fill[p] = 0
        for s in range(cap):
            req_ref[p, 0, s] = -1
        return carry

    lax.fori_loop(0, D, clear, 0)

    def lists(i, total):
        start_ref[i] = total
        for a in range(A):
            count = count_ref[i * A + a]
            for n in range(M):
                e = (i * A + a) * M + n
                dest = dest_ref[e]
                owner = lax.div(dest, B)
                block = dest - owner * B
                used = n < count
                look_ref[e] = jnp.where(used & (owner == me), block, -1)
                far = used & (owner != me)

                @pl.when(far)
                def _():
                    s = fill[owner]
                    req_ref[owner, 0, s] = block
                    fill[owner] = s + 1
                    act_ref[total] = a
                    pos_ref[total] = n
                    slot_ref[total] = owner * cap + s

                total = total + far.astype(jnp.int32)
        return total

    start_ref[B] = lax.fori_loop(0, B, lists, 0)


def greet(axis, others):
    barrier = pltpu.get_barrier_semaphore()
    for ids in others:
        pl.semaphore_signal(barrier, inc=1, device_id=ids, device_id_type=MESH)
    pl.semaphore_wait(barrier, len(others))


def request_kernel(D, req_ref, out_ref, land, send, recv):
    me = lax.axis_index("state")
    peers = [{"state": lax.rem(me + k, D)} for k in range(1, D)]
    greet("state", peers)
    copies = []
    for k in range(1, D):
        c = pltpu.make_async_remote_copy(
            src_ref=req_ref.at[lax.rem(me + k, D)],
            dst_ref=land.at[k],
            send_sem=send.at[k],
            recv_sem=recv.at[k],
            device_id={"state": lax.rem(me + k, D)},
            device_id_type=MESH,
        )
        c.start()
        copies.append(c)
    for c in copies:
        c.wait()
    out_ref[me] = req_ref[me]
    for k in range(1, D):
        out_ref[lax.rem(me - k + D, D)] = land[k]


def gather_kernel(D, cap, want_ref, val_ref, out_ref, sem):
    def copy(p, s):
        w = jnp.maximum(want_ref[p, 0, s], 0)
        return pltpu.make_async_copy(val_ref.at[w], out_ref.at[p * cap + s], sem.at[p * cap + s])

    def start(p, carry):
        for s in range(cap):
            copy(p, s).start()
        return carry

    def wait(p, carry):
        for s in range(cap):
            copy(p, s).wait()
        return carry

    lax.fori_loop(0, D, start, 0)
    lax.fori_loop(0, D, wait, 0)


def near_kernel(A, M, look_ref, val_ref, tiles_ref, cont_ref):
    i = pl.program_id(0)
    for a in range(A):
        weights, values = [], []
        for n in range(M):
            block = look_ref[(i * A + a) * M + n]
            keep = jnp.where(block >= 0, 1.0, 0.0).astype(jnp.float32)
            tile = tiles_ref[0, a, n]
            weights.append(tile * jnp.full(tile.shape, keep, jnp.float32).astype(jnp.bfloat16))
            values.append(val_ref[jnp.maximum(block, 0)])
        cont_ref[0, a] = jnp.dot(
            jnp.concatenate(weights, axis=1),
            jnp.concatenate(values, axis=0),
            preferred_element_type=jnp.float32,
        )


def transposed_dot(tile, right):
    return lax.dot_general(tile, right, (((0,), (0,)), ((), ())), preferred_element_type=jnp.float32)


def value_kernel(
    rows, start_ref, act_ref, pos_ref, slot_ref, cont_ref, inc_ref, tiles_ref, cot_ref, util_ref, taste_ref,
    value_ref, scaled_ref, out_ref, gu_ref, gt_ref, acc,
):
    i = pl.program_id(0)
    first, last = start_ref[i], start_ref[i + 1]
    acc[...] = cont_ref[0]

    def far(r, carry):
        a = act_ref[r]
        acc[a] += jnp.dot(
            tiles_ref[0, a, pos_ref[r]], inc_ref[slot_ref[r]], preferred_element_type=jnp.float32
        )
        return carry

    lax.fori_loop(first, last, far, 0)

    @pl.when(i == 0)
    def _():
        gt_ref[...] = jnp.zeros_like(gt_ref)

    tile_rows, width = cot_ref.shape
    t0, t1 = taste_ref[0:1, :], taste_ref[1:2, :]

    def chunk(c, carry):
        g0, g1 = carry
        at = pl.ds(pl.multiple_of(c * rows, rows), rows)
        util = util_ref[0, at, :]
        q0 = util[:, 0:1] + t0 + 0.95 * acc[0, at, :]
        q1 = util[:, 1:2] + t1 + 0.95 * acc[1, at, :]
        gap = q1 - q0
        small = jnp.exp(-jnp.abs(gap))
        total = 1.0 + small
        value_ref[at, :] = jnp.maximum(q0, q1) + jnp.log(total)
        big = cot_ref[at, :].astype(jnp.float32) / total
        little = big * small
        first_wins = gap <= 0.0
        h0 = jnp.where(first_wins, big, little)
        h1 = jnp.where(first_wins, little, big)
        scaled_ref[0, 0, at, :] = (0.95 * h0).astype(jnp.bfloat16)
        scaled_ref[0, 1, at, :] = (0.95 * h1).astype(jnp.bfloat16)
        gu_ref[0, at, 0:1] = jnp.sum(h0, axis=1, keepdims=True)
        gu_ref[0, at, 1:2] = jnp.sum(h1, axis=1, keepdims=True)
        return g0 + h0, g1 + h1

    zero = jnp.zeros((rows, width), jnp.float32)
    g0, g1 = lax.fori_loop(0, tile_rows // rows, chunk, (zero, zero))
    gt_ref[0:1, :] += jnp.sum(g0, axis=0, keepdims=True)
    gt_ref[1:2, :] += jnp.sum(g1, axis=0, keepdims=True)

    def back(r, carry):
        a = act_ref[r]
        out_ref[slot_ref[r]] = transposed_dot(tiles_ref[0, a, pos_ref[r]], scaled_ref[0, a]).astype(jnp.bfloat16)
        return carry

    lax.fori_loop(first, last, back, 0)


def back_kernel(A, M, look_ref, tiles_ref, scaled_ref, adj_ref):
    i = pl.program_id(0)

    @pl.when(i == 0)
    def _():
        adj_ref[...] = jnp.zeros_like(adj_ref)

    for a in range(A):
        for n in range(M):
            block = look_ref[(i * A + a) * M + n]

            @pl.when(block >= 0)
            def _():
                adj_ref[block] += transposed_dot(tiles_ref[0, a, n], scaled_ref[0, a])


def sums_kernel(D, T, gu_ref, gt_ref, ou_ref, ot_ref, lu, lt, us, ur, ts, tr):
    ms, mt = lax.axis_index("state"), lax.axis_index("type")
    peers = [{"state": lax.rem(ms + k, D)} for k in range(1, D)]
    peers += [{"type": lax.rem(mt + k, T)} for k in range(1, T)]
    greet("state", peers)
    copies = []
    for k in range(1, T):
        copies.append(
            pltpu.make_async_remote_copy(
                src_ref=gu_ref, dst_ref=lu.at[k], send_sem=us.at[k], recv_sem=ur.at[k],
                device_id={"type": lax.rem(mt + k, T)}, device_id_type=MESH,
            )
        )
    for k in range(1, D):
        copies.append(
            pltpu.make_async_remote_copy(
                src_ref=gt_ref, dst_ref=lt.at[k], send_sem=ts.at[k], recv_sem=tr.at[k],
                device_id={"state": lax.rem(ms + k, D)}, device_id_type=MESH,
            )
        )
    for c in copies:
        c.start()
    for c in copies:
        c.wait()
    lu[0] = gu_ref[...]
    lt[0] = gt_ref[...]
    u = lu[lax.rem(mt, T)]
    for j in range(1, T):
        u = u + lu[lax.rem(mt - j + T, T)]
    t = lt[lax.rem(ms, D)]
    for j in range(1, D):
        t = t + lt[lax.rem(ms - j + D, D)]
    ou_ref[...] = u
    ot_ref[...] = t


def land_kernel(D, cap, want_ref, adj_ref, ret_ref, out_ref):
    j = pl.program_id(0)
    out_ref[...] = adj_ref[...]

    def peer(p, carry):
        for s in range(cap):

            @pl.when(want_ref[p, 0, s] == j)
            def _():
                out_ref[0] += ret_ref[p * cap + s].astype(jnp.float32)

        return carry

    lax.fori_loop(0, D, peer, 0)


def local(value_in, cotangent, state_util, taste, tiles, dest_block, counts):
    B, A, M, R, _ = tiles.shape
    W = value_in.shape[1]
    D = lax.axis_size("state")
    T = lax.axis_size("type")
    cap = max(2, (B + D - 2) // (D - 1))
    E, C = B * A * M, D * cap
    f32, bf16, i32 = jnp.float32, jnp.bfloat16, jnp.int32
    shape = jax.ShapeDtypeStruct
    values = value_in.reshape(B, R, W)

    req, look, start, act, pos, slot = pl.pallas_call(
        functools.partial(plan_kernel, (B, A, M, D, cap)),
        out_shape=(
            shape((D, 1, 128), i32), shape((E,), i32), shape((B + 1,), i32),
            shape((C,), i32), shape((C,), i32), shape((C,), i32),
        ),
        in_specs=[smem()] * 3,
        out_specs=[smem()] * 6,
        scratch_shapes=[SMEM((D,), i32)],
        name="plan",
    )(lax.axis_index("state").reshape(1).astype(i32), dest_block.reshape(E), counts.reshape(B * A))

    wanted = pl.pallas_call(
        functools.partial(request_kernel, D),
        out_shape=shape((D, 1, 128), i32),
        in_specs=[pl.BlockSpec(memory_space=VMEM)],
        out_specs=pl.BlockSpec(memory_space=VMEM),
        scratch_shapes=[VMEM((D, 1, 128), i32), pltpu.SemaphoreType.DMA((D,)), pltpu.SemaphoreType.DMA((D,))],
        compiler_params=pltpu.CompilerParams(collective_id=0, has_side_effects=True),
        name="request",
    )(req)

    outgoing = pl.pallas_call(
        functools.partial(gather_kernel, D, cap),
        out_shape=shape((C, R, W), bf16),
        in_specs=[smem(), pl.BlockSpec(memory_space=VMEM)],
        out_specs=pl.BlockSpec(memory_space=pl.ANY),
        scratch_shapes=[pltpu.SemaphoreType.DMA((C,))],
        name="gather",
    )(wanted, values)

    incoming = lax.all_to_all(
        outgoing.reshape(D, cap, R, W), "state", split_axis=0, concat_axis=0, tiled=True
    ).reshape(C, R, W)

    tile_spec = pl.BlockSpec((1, A, M, R, R), lambda i: (i, 0, 0, 0, 0))
    pair_spec = pl.BlockSpec((1, A, R, W), lambda i: (i, 0, 0, 0))
    row_spec = pl.BlockSpec((R, W), lambda i: (i, 0))
    flops = 2 * E * R * R * W

    cont = pl.pallas_call(
        functools.partial(near_kernel, A, M),
        grid=(B,),
        out_shape=shape((B, A, R, W), f32),
        in_specs=[smem(), whole((B, R, W)), tile_spec],
        out_specs=pair_spec,
        cost_estimate=pl.CostEstimate(flops=flops, bytes_accessed=16 << 20, transcendentals=0),
        name="near",
    )(look, values, tiles)

    util_cols = state_util.reshape(A, B, R).transpose(1, 2, 0)
    value, scaled, outbound, gu, gt = pl.pallas_call(
        functools.partial(value_kernel, 16),
        grid=(B,),
        out_shape=(
            shape((B * R, W), f32), shape((B, A, R, W), bf16), shape((C, R, W), bf16),
            shape((B, R, A), f32), shape((A, W), f32),
        ),
        in_specs=[smem()] * 4
        + [
            pair_spec, whole((C, R, W)), tile_spec, row_spec,
            pl.BlockSpec((1, R, A), lambda i: (i, 0, 0)), whole((A, W)),
        ],
        out_specs=[
            row_spec, pair_spec, whole((C, R, W)), pl.BlockSpec((1, R, A), lambda i: (i, 0, 0)), whole((A, W)),
        ],
        scratch_shapes=[VMEM((A, R, W), f32)],
        cost_estimate=pl.CostEstimate(flops=flops // 4, bytes_accessed=30 << 20, transcendentals=3 * B * R * W),
        name="value",
    )(start, act, pos, slot, cont, incoming, tiles, cotangent, util_cols, taste)

    returned = lax.all_to_all(
        outbound.reshape(D, cap, R, W), "state", split_axis=0, concat_axis=0, tiled=True
    ).reshape(C, R, W)

    adj = pl.pallas_call(
        functools.partial(back_kernel, A, M),
        grid=(B,),
        out_shape=shape((B, R, W), f32),
        in_specs=[smem(), tile_spec, pair_spec],
        out_specs=whole((B, R, W)),
        cost_estimate=pl.CostEstimate(flops=flops, bytes_accessed=14 << 20, transcendentals=0),
        name="back",
    )(look, tiles, scaled)

    gu_rows = gu.transpose(2, 0, 1).reshape(A, B * R) / (W * T)
    grad_util, grad_taste = pl.pallas_call(
        functools.partial(sums_kernel, D, T),
        out_shape=(shape((A, B * R), f32), shape((A, W), f32)),
        in_specs=[pl.BlockSpec(memory_space=VMEM)] * 2,
        out_specs=[pl.BlockSpec(memory_space=VMEM)] * 2,
        scratch_shapes=[
            VMEM((T, A, B * R), f32), VMEM((D, A, W), f32),
            pltpu.SemaphoreType.DMA((T,)), pltpu.SemaphoreType.DMA((T,)),
            pltpu.SemaphoreType.DMA((D,)), pltpu.SemaphoreType.DMA((D,)),
        ],
        compiler_params=pltpu.CompilerParams(collective_id=1, has_side_effects=True),
        cost_estimate=pl.CostEstimate(flops=0, bytes_accessed=8 << 20, transcendentals=0),
        name="sums",
    )(gu_rows, gt / (B * R * D))

    block_spec = pl.BlockSpec((1, R, W), lambda j: (j, 0, 0))
    adjoint = pl.pallas_call(
        functools.partial(land_kernel, D, cap),
        grid=(B,),
        out_shape=shape((B, R, W), f32),
        in_specs=[smem(), block_spec, whole((C, R, W))],
        out_specs=block_spec,
        name="land",
    )(wanted, adj, returned)
    return value, adjoint.reshape(B * R, W), grad_util, grad_taste


def solution(mesh):
    rows = ("groups", "state")
    return jax.shard_map(
        local,
        mesh=mesh,
        in_specs=(
            P(rows, "type"),
            P(rows, "type"),
            P(None, rows),
            P(None, ("groups", "type")),
            P(rows, None, None, None, None),
            P(rows, None, None),
            P(rows, None),
        ),
        out_specs=(P(rows, "type"), P(rows, "type"), P(None, rows), P(None, ("groups", "type"))),
        check_vma=False,
    )
```

```python
import functools

import jax
import jax.numpy as jnp
from jax import lax
from jax.experimental import pallas as pl
from jax.experimental.pallas import tpu as pltpu
from jax.sharding import PartitionSpec as P

VMEM = pltpu.VMEM
SMEM = pltpu.SMEM
MESH = pl.DeviceIdType.MESH


def smem():
    return pl.BlockSpec(memory_space=SMEM)


def whole(shape):
    return pl.BlockSpec(shape, lambda *g: (0,) * len(shape))


def plan_kernel(dims, me_ref, dest_ref, count_ref, req_ref, look_ref, start_ref, act_ref, pos_ref, slot_ref, fill):
    B, A, M, D, cap = dims
    me = me_ref[0]

    def clear(p, carry):
        fill[p] = 0
        for s in range(cap):
            req_ref[p, 0, s] = -1
        return carry

    lax.fori_loop(0, D, clear, 0)

    def lists(i, total):
        start_ref[i] = total
        for a in range(A):
            count = count_ref[a, i]
            for n in range(M):
                e = (i * A + a) * M + n
                dest = dest_ref[n, a, i]
                owner = lax.div(dest, B)
                block = dest - owner * B
                used = n < count
                look_ref[e] = jnp.where(used & (owner == me), block, -1)
                far = used & (owner != me)

                @pl.when(far)
                def _():
                    s = fill[owner]
                    req_ref[owner, 0, s] = block
                    fill[owner] = s + 1
                    act_ref[total] = a
                    pos_ref[total] = n
                    slot_ref[total] = owner * cap + s

                total = total + far.astype(jnp.int32)
        return total

    start_ref[B] = lax.fori_loop(0, B, lists, 0)


def greet(axis, others):
    barrier = pltpu.get_barrier_semaphore()
    for ids in others:
        pl.semaphore_signal(barrier, inc=1, device_id=ids, device_id_type=MESH)
    pl.semaphore_wait(barrier, len(others))


def request_kernel(D, req_ref, out_ref, land, send, recv):
    me = lax.axis_index("state")
    peers = [{"state": lax.rem(me + k, D)} for k in range(1, D)]
    greet("state", peers)
    copies = []
    for k in range(1, D):
        c = pltpu.make_async_remote_copy(
            src_ref=req_ref.at[lax.rem(me + k, D)],
            dst_ref=land.at[k],
            send_sem=send.at[k],
            recv_sem=recv.at[k],
            device_id={"state": lax.rem(me + k, D)},
            device_id_type=MESH,
        )
        c.start()
        copies.append(c)
    for c in copies:
        c.wait()
    out_ref[me] = req_ref[me]
    for k in range(1, D):
        out_ref[lax.rem(me - k + D, D)] = land[k]


def gather_kernel(D, cap, half, want_ref, val_ref, *rest):
    outs, sem = rest[:-1], rest[-1]

    def run(h, act):
        def peer(p, carry):
            for s in range(cap):
                w = jnp.maximum(want_ref[p, 0, s], 0)
                act(
                    pltpu.make_async_copy(
                        val_ref.at[w, :, pl.ds(h * half, half)],
                        outs[h].at[p * cap + s],
                        sem.at[h, p * cap + s],
                    )
                )
            return carry

        lax.fori_loop(0, D, peer, 0)

    for h in range(len(outs)):
        run(h, lambda c: c.start())
    for h in range(len(outs)):
        run(h, lambda c: c.wait())


def near_kernel(G, A, M, look_ref, val_ref, tiles_ref, cont_ref):
    for g in range(G):
        i = pl.program_id(0) * G + g
        for a in range(A):
            weights, values = [], []
            for n in range(M):
                block = look_ref[(i * A + a) * M + n]
                keep = jnp.where(block >= 0, 1.0, 0.0).astype(jnp.float32)
                tile = tiles_ref[g, a, n]
                weights.append(tile * jnp.full(tile.shape, keep, jnp.float32).astype(jnp.bfloat16))
                values.append(val_ref[jnp.maximum(block, 0)])
            cont_ref[g, a] = jnp.dot(
                jnp.concatenate(weights, axis=1),
                jnp.concatenate(values, axis=0),
                preferred_element_type=jnp.float32,
            )


def transposed_dot(tile, right):
    return lax.dot_general(tile, right, (((0,), (0,)), ((), ())), preferred_element_type=jnp.float32)


def value_kernel(
    G, rows, start_ref, act_ref, pos_ref, slot_ref, cont_ref, inc_ref, tiles_ref, cot_ref, util_ref, taste_ref, *rest
):
    value_ref, scaled_ref, out_ref, gu_ref, gt_ref, acc = rest[-6:]
    step = pl.program_id(0)

    @pl.when(step == 0)
    def _():
        gt_ref[...] = jnp.zeros_like(gt_ref)

    R = tiles_ref.shape[3]
    acc[...] = cont_ref[...]
    t0, t1 = taste_ref[0:1, :], taste_ref[1:2, :]
    for g in range(G):
        i = step * G + g

        def far(r, carry):
            a = act_ref[r]
            acc[g, a] += jnp.dot(
                tiles_ref[g, a, pos_ref[r]], inc_ref[slot_ref[r]], preferred_element_type=jnp.float32
            )
            return carry

        lax.fori_loop(start_ref[i], start_ref[i + 1], far, 0)
    for g in range(G):
        g0 = g1 = 0.0
        for c in range(0, R, rows):
            at = slice(c, c + rows)
            here = slice(g * R + c, g * R + c + rows)
            util = util_ref[g, at, :]
            q0 = util[:, 0:1] + t0 + 0.95 * acc[g, 0, at, :]
            q1 = util[:, 1:2] + t1 + 0.95 * acc[g, 1, at, :]
            gap = q1 - q0
            small = jnp.exp(-jnp.abs(gap))
            total = 1.0 + small
            value_ref[here, :] = jnp.maximum(q0, q1) + jnp.log(total)
            big = cot_ref[here, :].astype(jnp.float32) / total
            little = big * small
            first_wins = gap <= 0.0
            h0 = jnp.where(first_wins, big, little)
            h1 = jnp.where(first_wins, little, big)
            scaled_ref[g, 0, at, :] = (0.95 * h0).astype(jnp.bfloat16)
            scaled_ref[g, 1, at, :] = (0.95 * h1).astype(jnp.bfloat16)
            gu_ref[g, at, 0:1] = jnp.sum(h0, axis=1, keepdims=True)
            gu_ref[g, at, 1:2] = jnp.sum(h1, axis=1, keepdims=True)
            g0, g1 = g0 + h0, g1 + h1
        gt_ref[0:1, :] += jnp.sum(g0, axis=0, keepdims=True)
        gt_ref[1:2, :] += jnp.sum(g1, axis=0, keepdims=True)
    for g in range(G):
        i = step * G + g

        def back(r, carry):
            a = act_ref[r]
            out_ref[slot_ref[r]] = transposed_dot(tiles_ref[g, a, pos_ref[r]], scaled_ref[g, a]).astype(jnp.bfloat16)
            return carry

        lax.fori_loop(start_ref[i], start_ref[i + 1], back, 0)


def back_kernel(G, A, M, look_ref, tiles_ref, scaled_ref, adj_ref):
    step = pl.program_id(0)

    @pl.when(step == 0)
    def _():
        adj_ref[...] = jnp.zeros_like(adj_ref)

    for g in range(G):
        i = step * G + g
        for a in range(A):
            for n in range(M):
                block = look_ref[(i * A + a) * M + n]

                @pl.when(block >= 0)
                def _():
                    adj_ref[block] += transposed_dot(tiles_ref[g, a, n], scaled_ref[g, a])


def sums_kernel(D, T, gu_ref, gt_ref, after_ref, ou_ref, ot_ref, lu, lt, us, ur, ts, tr):
    ms, mt = lax.axis_index("state"), lax.axis_index("type")
    peers = [{"state": lax.rem(ms + k, D)} for k in range(1, D)]
    peers += [{"type": lax.rem(mt + k, T)} for k in range(1, T)]
    greet("state", peers)
    copies = []
    for k in range(1, T):
        copies.append(
            pltpu.make_async_remote_copy(
                src_ref=gu_ref, dst_ref=lu.at[k], send_sem=us.at[k], recv_sem=ur.at[k],
                device_id={"type": lax.rem(mt + k, T)}, device_id_type=MESH,
            )
        )
    for k in range(1, D):
        copies.append(
            pltpu.make_async_remote_copy(
                src_ref=gt_ref, dst_ref=lt.at[k], send_sem=ts.at[k], recv_sem=tr.at[k],
                device_id={"state": lax.rem(ms + k, D)}, device_id_type=MESH,
            )
        )
    for c in copies:
        c.start()
    for c in copies:
        c.wait()
    lu[0] = gu_ref[...]
    lt[0] = gt_ref[...]
    u = lu[lax.rem(mt, T)]
    for j in range(1, T):
        u = u + lu[lax.rem(mt - j + T, T)]
    t = lt[lax.rem(ms, D)]
    for j in range(1, D):
        t = t + lt[lax.rem(ms - j + D, D)]
    ou_ref[...] = u
    ot_ref[...] = t


def land_kernel(D, cap, want_ref, adj_ref, ret_ref, *rest):
    out_ref = rest[-1]
    out_ref[...] = adj_ref[...]

    def peer(p, carry):
        for s in range(cap):
            w = want_ref[p, 0, s]

            @pl.when(w >= 0)
            def _():
                out_ref[w] += ret_ref[p * cap + s].astype(jnp.float32)

        return carry

    lax.fori_loop(0, D, peer, 0)


def local(value_in, cotangent, state_util, taste, tiles, dest_block, counts):
    B, A, M, R, _ = tiles.shape
    W = value_in.shape[1]
    D = lax.axis_size("state")
    T = lax.axis_size("type")
    cap = max(2, (B + D - 2) // (D - 1))
    E, C = B * A * M, D * cap
    f32, bf16, i32 = jnp.float32, jnp.bfloat16, jnp.int32
    shape = jax.ShapeDtypeStruct
    values = value_in.reshape(B, R, W)

    req, look, start, act, pos, slot = pl.pallas_call(
        functools.partial(plan_kernel, (B, A, M, D, cap)),
        out_shape=(
            shape((D, 1, 128), i32), shape((E,), i32), shape((B + 1,), i32),
            shape((C,), i32), shape((C,), i32), shape((C,), i32),
        ),
        in_specs=[smem()] * 3,
        out_specs=[smem()] * 6,
        scratch_shapes=[SMEM((D,), i32)],
        name="plan",
    )(lax.axis_index("state").reshape(1).astype(i32), dest_block.transpose(2, 1, 0), counts.T)

    wanted = pl.pallas_call(
        functools.partial(request_kernel, D),
        out_shape=shape((D, 1, 128), i32),
        in_specs=[pl.BlockSpec(memory_space=VMEM)],
        out_specs=pl.BlockSpec(memory_space=VMEM),
        scratch_shapes=[VMEM((D, 1, 128), i32), pltpu.SemaphoreType.DMA((D,)), pltpu.SemaphoreType.DMA((D,))],
        compiler_params=pltpu.CompilerParams(collective_id=0, has_side_effects=True),
        name="request",
    )(req)

    H = 2 if W % 256 == 0 else 1
    V = W // H
    G = 4 if B % 4 == 0 else 1
    outgoing = pl.pallas_call(
        functools.partial(gather_kernel, D, cap, V),
        out_shape=tuple(shape((C, R, V), bf16) for h in range(H)),
        in_specs=[smem(), pl.BlockSpec(memory_space=VMEM)],
        out_specs=[pl.BlockSpec(memory_space=pl.ANY)] * H,
        scratch_shapes=[pltpu.SemaphoreType.DMA((H, C))],
        name="gather",
    )(wanted, values)

    def exchange(x):
        return lax.all_to_all(
            x.reshape(D, cap, R, V), "state", split_axis=0, concat_axis=0, tiled=True
        ).reshape(C, R, V)

    incoming = [exchange(x) for x in outgoing]

    flops = 2 * E * R * R * W
    cont = pl.pallas_call(
        functools.partial(near_kernel, G, A, M),
        grid=(B // G,),
        out_shape=shape((B, A, R, W), f32),
        in_specs=[smem(), whole((B, R, W)), pl.BlockSpec((G, A, M, R, R), lambda i: (i, 0, 0, 0, 0))],
        out_specs=pl.BlockSpec((G, A, R, W), lambda i: (i, 0, 0, 0)),
        cost_estimate=pl.CostEstimate(flops=flops, bytes_accessed=16 << 20, transcendentals=0),
        name="near",
    )(look, values, tiles)

    util_cols = state_util.reshape(A, B, R).transpose(1, 2, 0)
    value = scaled = None
    gus, gts, outbound = [], [], []
    for h in range(H):
        held = [] if h == 0 else [value, scaled]
        value, scaled, out, gu, gt = pl.pallas_call(
            functools.partial(value_kernel, G, 32),
            grid=(B // G,),
            out_shape=(
                shape((B * R, W), f32), shape((B, A, R, W), bf16), shape((C, R, V), bf16),
                shape((B, R, A), f32), shape((A, V), f32),
            ),
            in_specs=[smem()] * 4
            + [
                pl.BlockSpec((G, A, R, V), lambda i, h=h: (i, 0, 0, h)),
                whole((C, R, V)),
                pl.BlockSpec((G, A, M, R, R), lambda i: (i, 0, 0, 0, 0)),
                pl.BlockSpec((G * R, V), lambda i, h=h: (i, h)),
                pl.BlockSpec((G, R, A), lambda i: (i, 0, 0)),
                pl.BlockSpec((A, V), lambda i, h=h: (0, h)),
            ]
            + [pl.BlockSpec(memory_space=pl.ANY)] * len(held),
            out_specs=[
                pl.BlockSpec((G * R, V), lambda i, h=h: (i, h)),
                pl.BlockSpec((G, A, R, V), lambda i, h=h: (i, 0, 0, h)),
                whole((C, R, V)),
                pl.BlockSpec((G, R, A), lambda i: (i, 0, 0)),
                whole((A, V)),
            ],
            input_output_aliases={10 + k: k for k in range(len(held))},
            scratch_shapes=[VMEM((G, A, R, V), f32)],
            cost_estimate=pl.CostEstimate(
                flops=flops // (4 * H), bytes_accessed=(30 << 20) // H, transcendentals=3 * B * R * V
            ),
            name="value",
        )(start, act, pos, slot, cont, incoming[h], tiles, cotangent, util_cols, taste, *held)
        outbound.append(out)
        gus.append(gu)
        gts.append(gt)

    returned = [exchange(x) for x in outbound]

    adj = pl.pallas_call(
        functools.partial(back_kernel, G, A, M),
        grid=(B // G,),
        out_shape=shape((B, R, W), f32),
        in_specs=[
            smem(),
            pl.BlockSpec((G, A, M, R, R), lambda i: (i, 0, 0, 0, 0)),
            pl.BlockSpec((G, A, R, W), lambda i: (i, 0, 0, 0)),
        ],
        out_specs=whole((B, R, W)),
        cost_estimate=pl.CostEstimate(flops=flops, bytes_accessed=14 << 20, transcendentals=0),
        name="back",
    )(look, tiles, scaled)

    gu_rows = sum(gus).transpose(2, 0, 1).reshape(A, B * R) / (W * T)
    grad_util, grad_taste = pl.pallas_call(
        functools.partial(sums_kernel, D, T),
        out_shape=(shape((A, B * R), f32), shape((A, W), f32)),
        in_specs=[pl.BlockSpec(memory_space=VMEM)] * 2 + [pl.BlockSpec(memory_space=pl.ANY)],
        out_specs=[pl.BlockSpec(memory_space=VMEM)] * 2,
        scratch_shapes=[
            VMEM((T, A, B * R), f32), VMEM((D, A, W), f32),
            pltpu.SemaphoreType.DMA((T,)), pltpu.SemaphoreType.DMA((T,)),
            pltpu.SemaphoreType.DMA((D,)), pltpu.SemaphoreType.DMA((D,)),
        ],
        compiler_params=pltpu.CompilerParams(collective_id=1, has_side_effects=True),
        cost_estimate=pl.CostEstimate(flops=0, bytes_accessed=8 << 20, transcendentals=0),
        name="sums",
    )(gu_rows, jnp.concatenate(gts, axis=1) / (B * R * D), adj)

    adjoint = adj
    for h in range(H):
        adjoint = pl.pallas_call(
            functools.partial(land_kernel, D, cap),
            grid=(1,),
            out_shape=shape((B, R, W), f32),
            in_specs=[smem(), pl.BlockSpec((B, R, V), lambda j, h=h: (0, 0, h)), whole((C, R, V))],
            out_specs=pl.BlockSpec((B, R, V), lambda j, h=h: (0, 0, h)),
            input_output_aliases={1: 0},
            name="land",
        )(wanted, adjoint, returned[h])
    return value, adjoint.reshape(B * R, W), grad_util, grad_taste


def solution(mesh):
    rows = ("groups", "state")
    return jax.shard_map(
        local,
        mesh=mesh,
        in_specs=(
            P(rows, "type"),
            P(rows, "type"),
            P(None, rows),
            P(None, ("groups", "type")),
            P(rows, None, None, None, None),
            P(rows, None, None),
            P(rows, None),
        ),
        out_specs=(P(rows, "type"), P(rows, "type"), P(None, rows), P(None, ("groups", "type"))),
        check_vma=False,
    )
```

```python
import functools

import jax
import jax.numpy as jnp
from jax import lax
from jax.experimental import pallas as pl
from jax.experimental.pallas import tpu as pltpu
from jax.sharding import PartitionSpec as P

VMEM = pltpu.VMEM
SMEM = pltpu.SMEM
MESH = pl.DeviceIdType.MESH


def smem():
    return pl.BlockSpec(memory_space=SMEM)


def whole(shape):
    return pl.BlockSpec(shape, lambda *g: (0,) * len(shape))


def plan_kernel(dims, me_ref, dest_ref, count_ref, req_ref, look_ref, from_ref, fill):
    B, A, M, D, cap = dims
    me = me_ref[0]

    def clear(p, carry):
        fill[p] = 0
        for s in range(cap):
            req_ref[p, 0, s] = -1
            from_ref[p * cap + s] = 0
        return carry

    lax.fori_loop(0, D, clear, 0)

    def lists(i, carry):
        for a in range(A):
            count = count_ref[a, i]
            for n in range(M):
                e = (i * A + a) * M + n
                dest = dest_ref[n, a, i]
                owner = lax.div(dest, B)
                block = dest - owner * B
                used = n < count
                look_ref[e] = jnp.where(used & (owner == me), block, -1)

                @pl.when(used & (owner != me))
                def _():
                    s = fill[owner]
                    fill[owner] = s + 1
                    req_ref[owner, 0, s] = block
                    from_ref[owner * cap + s] = e
                    look_ref[e] = B + owner * cap + s

        return carry

    lax.fori_loop(0, B, lists, 0)


def greet(axis, others):
    barrier = pltpu.get_barrier_semaphore()
    for ids in others:
        pl.semaphore_signal(barrier, inc=1, device_id=ids, device_id_type=MESH)
    pl.semaphore_wait(barrier, len(others))


def request_kernel(D, req_ref, out_ref, land, send, recv):
    me = lax.axis_index("state")
    peers = [{"state": lax.rem(me + k, D)} for k in range(1, D)]
    greet("state", peers)
    copies = []
    for k in range(1, D):
        c = pltpu.make_async_remote_copy(
            src_ref=req_ref.at[lax.rem(me + k, D)],
            dst_ref=land.at[k],
            send_sem=send.at[k],
            recv_sem=recv.at[k],
            device_id={"state": lax.rem(me + k, D)},
            device_id_type=MESH,
        )
        c.start()
        copies.append(c)
    for c in copies:
        c.wait()
    out_ref[me] = req_ref[me]
    for k in range(1, D):
        out_ref[lax.rem(me - k + D, D)] = land[k]


def gather_kernel(D, cap, half, want_ref, val_ref, *rest):
    outs, sem = rest[:-1], rest[-1]

    def run(h, act):
        def peer(p, carry):
            for s in range(cap):
                w = jnp.maximum(want_ref[p, 0, s], 0)
                act(
                    pltpu.make_async_copy(
                        val_ref.at[w, :, pl.ds(h * half, half)],
                        outs[h].at[p * cap + s],
                        sem.at[h, p * cap + s],
                    )
                )
            return carry

        lax.fori_loop(0, D, peer, 0)

    for h in range(len(outs)):
        run(h, lambda c: c.start())
    for h in range(len(outs)):
        run(h, lambda c: c.wait())


def transposed_dot(tile, right):
    return lax.dot_general(tile, right, (((0,), (0,)), ((), ())), preferred_element_type=jnp.float32)


def continuation(M, first, look_ref, table, tiles):
    weights, values = [], []
    for n in range(M):
        row = look_ref[first + n]
        keep = jnp.where(row >= 0, 1.0, 0.0).astype(jnp.float32)
        tile = tiles(n)
        weights.append(tile * jnp.full(tile.shape, keep, jnp.float32).astype(jnp.bfloat16))
        values.append(table[jnp.maximum(row, 0)])
    return jnp.dot(
        jnp.concatenate(weights, axis=1), jnp.concatenate(values, axis=0), preferred_element_type=jnp.float32
    )


def value_kernel(
    G, rows, col, look_ref, from_ref, val_ref, inc_ref, tiles_ref, cot_ref, util_ref, taste_ref, *rest
):
    value_ref, scaled_ref, out_ref, gu_ref, gt_ref, acc, table, kept, sem = rest[-9:]
    step = pl.program_id(0)
    _, A, M, R, _ = tiles_ref.shape
    B, C, V = val_ref.shape[0], inc_ref.shape[0], inc_ref.shape[2]

    @pl.when(step == 0)
    def _():
        gt_ref[...] = jnp.zeros_like(gt_ref)
        own = pltpu.make_async_copy(val_ref.at[:, :, pl.ds(col, V)], table.at[pl.ds(0, B)], sem.at[0])
        far = pltpu.make_async_copy(inc_ref, table.at[pl.ds(B, C)], sem.at[1])
        own.start()
        far.start()
        own.wait()
        far.wait()

    t0, t1 = taste_ref[0:1, :], taste_ref[1:2, :]
    for g in range(G):
        i = step * G + g
        for a in range(A):
            acc[g, a] = continuation(M, (i * A + a) * M, look_ref, table, lambda n: tiles_ref[i, a, n])
    for g in range(G):
        g0 = g1 = 0.0
        for c in range(0, R, rows):
            at = slice(c, c + rows)
            here = slice(g * R + c, g * R + c + rows)
            util = util_ref[g, at, :]
            q0 = util[:, 0:1] + t0 + 0.95 * acc[g, 0, at, :]
            q1 = util[:, 1:2] + t1 + 0.95 * acc[g, 1, at, :]
            gap = q1 - q0
            small = jnp.exp(-jnp.abs(gap))
            total = 1.0 + small
            value_ref[here, :] = jnp.maximum(q0, q1) + jnp.log(total)
            big = cot_ref[here, :].astype(jnp.float32) / total
            little = big * small
            first_wins = gap <= 0.0
            h0 = jnp.where(first_wins, big, little)
            h1 = jnp.where(first_wins, little, big)
            scaled_ref[g, 0, at, :] = (0.95 * h0).astype(jnp.bfloat16)
            scaled_ref[g, 1, at, :] = (0.95 * h1).astype(jnp.bfloat16)
            gu_ref[g, at, 0:1] = jnp.sum(h0, axis=1, keepdims=True)
            gu_ref[g, at, 1:2] = jnp.sum(h1, axis=1, keepdims=True)
            g0, g1 = g0 + h0, g1 + h1
        gt_ref[0:1, :] += jnp.sum(g0, axis=0, keepdims=True)
        gt_ref[1:2, :] += jnp.sum(g1, axis=0, keepdims=True)
    kept[pl.ds(step * G, G)] = scaled_ref[...]

    @pl.when(step == pl.num_programs(0) - 1)
    def _():
        def back(q, carry):
            for u in range(2):
                slot = q * 2 + u
                e = from_ref[slot]
                pair = lax.div(e, M)
                i = lax.div(pair, A)
                a = pair - i * A
                out_ref[slot] = transposed_dot(tiles_ref[i, a, e - pair * M], kept[i, a]).astype(jnp.bfloat16)
            return carry

        lax.fori_loop(0, C // 2, back, 0)


def back_kernel(G, A, M, look_ref, tiles_ref, scaled_ref, adj_ref):
    step = pl.program_id(0)

    @pl.when(step == 0)
    def _():
        adj_ref[...] = jnp.zeros_like(adj_ref)

    for g in range(G):
        i = step * G + g
        for a in range(A):
            for n in range(M):
                block = look_ref[(i * A + a) * M + n]

                @pl.when((block >= 0) & (block < adj_ref.shape[0]))
                def _():
                    adj_ref[block] += transposed_dot(tiles_ref[g, a, n], scaled_ref[g, a])


def sums_kernel(D, T, gu_ref, gt_ref, token_ref, after_ref, ou_ref, ot_ref, lu, lt, us, ur, ts, tr):
    ms, mt = lax.axis_index("state"), lax.axis_index("type")
    peers = [{"state": lax.rem(ms + k, D)} for k in range(1, D)]
    peers += [{"type": lax.rem(mt + k, T)} for k in range(1, T)]
    greet("state", peers)
    copies = []
    for k in range(1, T):
        copies.append(
            pltpu.make_async_remote_copy(
                src_ref=gu_ref, dst_ref=lu.at[k], send_sem=us.at[k], recv_sem=ur.at[k],
                device_id={"type": lax.rem(mt + k, T)}, device_id_type=MESH,
            )
        )
    for k in range(1, D):
        copies.append(
            pltpu.make_async_remote_copy(
                src_ref=gt_ref, dst_ref=lt.at[k], send_sem=ts.at[k], recv_sem=tr.at[k],
                device_id={"state": lax.rem(ms + k, D)}, device_id_type=MESH,
            )
        )
    for c in copies:
        c.start()
    for c in copies:
        c.wait()
    lu[0] = gu_ref[...]
    lt[0] = gt_ref[...]
    u = lu[lax.rem(mt, T)]
    for j in range(1, T):
        u = u + lu[lax.rem(mt - j + T, T)]
    t = lt[lax.rem(ms, D)]
    for j in range(1, D):
        t = t + lt[lax.rem(ms - j + D, D)]
    ou_ref[...] = u
    ot_ref[...] = t


def land_kernel(D, cap, want_ref, adj_ref, ret_ref, *rest):
    out_ref, done_ref = rest[-2:]
    done_ref[0] = 0
    out_ref[...] = adj_ref[...]

    def peer(p, carry):
        for s in range(cap):
            w = want_ref[p, 0, s]

            @pl.when(w >= 0)
            def _():
                out_ref[w] += ret_ref[p * cap + s].astype(jnp.float32)

        return carry

    lax.fori_loop(0, D, peer, 0)


def local(value_in, cotangent, state_util, taste, tiles, dest_block, counts):
    B, A, M, R, _ = tiles.shape
    W = value_in.shape[1]
    D = lax.axis_size("state")
    T = lax.axis_size("type")
    cap = max(2, (B + D - 2) // (D - 1))
    E, C = B * A * M, D * cap
    f32, bf16, i32 = jnp.float32, jnp.bfloat16, jnp.int32
    shape = jax.ShapeDtypeStruct
    values = value_in.reshape(B, R, W)

    req, look, origin = pl.pallas_call(
        functools.partial(plan_kernel, (B, A, M, D, cap)),
        out_shape=(shape((D, 1, 128), i32), shape((E,), i32), shape((C,), i32)),
        in_specs=[smem()] * 3,
        out_specs=[smem()] * 3,
        scratch_shapes=[SMEM((D,), i32)],
        name="plan",
    )(lax.axis_index("state").reshape(1).astype(i32), dest_block.transpose(2, 1, 0), counts.T)

    wanted = pl.pallas_call(
        functools.partial(request_kernel, D),
        out_shape=shape((D, 1, 128), i32),
        in_specs=[pl.BlockSpec(memory_space=VMEM)],
        out_specs=pl.BlockSpec(memory_space=VMEM),
        scratch_shapes=[VMEM((D, 1, 128), i32), pltpu.SemaphoreType.DMA((D,)), pltpu.SemaphoreType.DMA((D,))],
        compiler_params=pltpu.CompilerParams(collective_id=0, has_side_effects=True),
        name="request",
    )(req)

    H = 2 if W % 256 == 0 else 1
    V = W // H
    G = 4 if B % 4 == 0 else 1
    outgoing = pl.pallas_call(
        functools.partial(gather_kernel, D, cap, V),
        out_shape=tuple(shape((C, R, V), bf16) for h in range(H)),
        in_specs=[smem(), pl.BlockSpec(memory_space=VMEM)],
        out_specs=[pl.BlockSpec(memory_space=pl.ANY)] * H,
        scratch_shapes=[pltpu.SemaphoreType.DMA((H, C))],
        name="gather",
    )(wanted, values)

    def exchange(x):
        return lax.all_to_all(
            x.reshape(D, cap, R, V), "state", split_axis=0, concat_axis=0, tiled=True
        ).reshape(C, R, V)

    incoming = [exchange(x) for x in outgoing]

    flops = 2 * E * R * R * W
    util_cols = state_util.reshape(A, B, R).transpose(1, 2, 0)
    value = None
    gus, gts, outbound, scaleds = [], [], [], []
    for h in range(H):
        held = [] if h == 0 else [value]
        value, scaled, out, gu, gt = pl.pallas_call(
            functools.partial(value_kernel, G, 32, h * V),
            grid=(B // G,),
            out_shape=(
                shape((B * R, W), f32), shape((B, A, R, V), bf16), shape((C, R, V), bf16),
                shape((B, R, A), f32), shape((A, V), f32),
            ),
            in_specs=[
                smem(), smem(), pl.BlockSpec(memory_space=pl.ANY), pl.BlockSpec(memory_space=pl.ANY),
                whole((B, A, M, R, R)),
                pl.BlockSpec((G * R, V), lambda i, h=h: (i, h)),
                pl.BlockSpec((G, R, A), lambda i: (i, 0, 0)),
                pl.BlockSpec((A, V), lambda i, h=h: (0, h)),
            ]
            + [pl.BlockSpec(memory_space=pl.ANY)] * len(held),
            out_specs=[
                pl.BlockSpec((G * R, V), lambda i, h=h: (i, h)),
                pl.BlockSpec((G, A, R, V), lambda i: (i, 0, 0, 0)),
                whole((C, R, V)),
                pl.BlockSpec((G, R, A), lambda i: (i, 0, 0)),
                whole((A, V)),
            ],
            input_output_aliases={8 + k: k for k in range(len(held))},
            scratch_shapes=[
                VMEM((G, A, R, V), f32), VMEM((B + C, R, V), bf16), VMEM((B, A, R, V), bf16),
                pltpu.SemaphoreType.DMA((2,)),
            ],
            cost_estimate=pl.CostEstimate(
                flops=flops // H, bytes_accessed=(24 << 20) // H, transcendentals=3 * B * R * V
            ),
            name="value",
        )(look, origin, values, incoming[h], tiles, cotangent, util_cols, taste, *held)
        outbound.append(out)
        scaleds.append(scaled)
        gus.append(gu)
        gts.append(gt)

    adjs = [
        pl.pallas_call(
            functools.partial(back_kernel, G, A, M),
            grid=(B // G,),
            out_shape=shape((B, R, V), f32),
            in_specs=[
                smem(),
                pl.BlockSpec((G, A, M, R, R), lambda i: (i, 0, 0, 0, 0)),
                pl.BlockSpec((G, A, R, V), lambda i: (i, 0, 0, 0)),
            ],
            out_specs=whole((B, R, V)),
            cost_estimate=pl.CostEstimate(flops=flops // H, bytes_accessed=(14 << 20) // H, transcendentals=0),
            name="back",
        )(look, tiles, x)
        for x in scaleds
    ]

    returned = []
    for h in range(H):
        if h > 0:
            outbound[h], adjs[h - 1] = lax.optimization_barrier((outbound[h], adjs[h - 1]))
        returned.append(exchange(outbound[h]))

    adjoint, tokens = None, []
    gu_rows = sum(gus).transpose(2, 0, 1).reshape(A, B * R) / (W * T)
    for h in range(H):
        held = [] if h == 0 else [adjoint]
        adjoint, token = pl.pallas_call(
            functools.partial(land_kernel, D, cap),
            grid=(1,),
            out_shape=(shape((B, R, W), f32), shape((1,), i32)),
            in_specs=[smem(), whole((B, R, V)), whole((C, R, V))]
            + [pl.BlockSpec(memory_space=pl.ANY)] * len(held),
            out_specs=[pl.BlockSpec((B, R, V), lambda j, h=h: (0, 0, h)), smem()],
            input_output_aliases={3 + k: k for k in range(len(held))},
            name="land",
        )(wanted, adjs[h], returned[h], *held)
        tokens.append(token)
    grad_util, grad_taste = pl.pallas_call(
        functools.partial(sums_kernel, D, T),
        out_shape=(shape((A, B * R), f32), shape((A, W), f32)),
        in_specs=[pl.BlockSpec(memory_space=VMEM)] * 2 + [smem(), pl.BlockSpec(memory_space=pl.ANY)],
        out_specs=[pl.BlockSpec(memory_space=VMEM)] * 2,
        scratch_shapes=[
            VMEM((T, A, B * R), f32), VMEM((D, A, W), f32),
            pltpu.SemaphoreType.DMA((T,)), pltpu.SemaphoreType.DMA((T,)),
            pltpu.SemaphoreType.DMA((D,)), pltpu.SemaphoreType.DMA((D,)),
        ],
        compiler_params=pltpu.CompilerParams(collective_id=1, has_side_effects=True),
        cost_estimate=pl.CostEstimate(flops=0, bytes_accessed=8 << 20, transcendentals=0),
        name="sums",
    )(gu_rows, jnp.concatenate(gts, axis=1) / (B * R * D), tokens[0], adjs[-1])

    return value, adjoint.reshape(B * R, W), grad_util, grad_taste


def solution(mesh):
    rows = ("groups", "state")
    return jax.shard_map(
        local,
        mesh=mesh,
        in_specs=(
            P(rows, "type"),
            P(rows, "type"),
            P(None, rows),
            P(None, ("groups", "type")),
            P(rows, None, None, None, None),
            P(rows, None, None),
            P(rows, None),
        ),
        out_specs=(P(rows, "type"), P(rows, "type"), P(None, rows), P(None, ("groups", "type"))),
        check_vma=False,
    )
```

```python
import functools

import jax
import jax.numpy as jnp
from jax import lax
from jax.experimental import pallas as pl
from jax.experimental.pallas import tpu as pltpu
from jax.sharding import PartitionSpec as P

VMEM = pltpu.VMEM
SMEM = pltpu.SMEM
MESH = pl.DeviceIdType.MESH


def smem():
    return pl.BlockSpec(memory_space=SMEM)


def whole(shape):
    return pl.BlockSpec(shape, lambda *g: (0,) * len(shape))


def plan_kernel(dims, me_ref, dest_ref, count_ref, req_ref, look_ref, from_ref, fill):
    B, A, M, D, cap = dims
    me = me_ref[0]

    def clear(p, carry):
        fill[p] = 0
        for s in range(cap):
            req_ref[p, 0, s] = -1
            from_ref[p * cap + s] = 0
        return carry

    lax.fori_loop(0, D, clear, 0)

    def lists(i, carry):
        for a in range(A):
            count = count_ref[a, i]
            for n in range(M):
                e = (i * A + a) * M + n
                dest = dest_ref[n, a, i]
                owner = lax.div(dest, B)
                block = dest - owner * B
                used = n < count
                look_ref[e] = jnp.where(used & (owner == me), block, -1)

                @pl.when(used & (owner != me))
                def _():
                    s = fill[owner]
                    fill[owner] = s + 1
                    req_ref[owner, 0, s] = block
                    from_ref[owner * cap + s] = e
                    look_ref[e] = B + owner * cap + s

        return carry

    lax.fori_loop(0, B, lists, 0)


def greet(axis, others):
    barrier = pltpu.get_barrier_semaphore()
    for ids in others:
        pl.semaphore_signal(barrier, inc=1, device_id=ids, device_id_type=MESH)
    pl.semaphore_wait(barrier, len(others))


def request_kernel(D, req_ref, out_ref, land, send, recv):
    me = lax.axis_index("state")
    peers = [{"state": lax.rem(me + k, D)} for k in range(1, D)]
    greet("state", peers)
    copies = []
    for k in range(1, D):
        c = pltpu.make_async_remote_copy(
            src_ref=req_ref.at[lax.rem(me + k, D)],
            dst_ref=land.at[k],
            send_sem=send.at[k],
            recv_sem=recv.at[k],
            device_id={"state": lax.rem(me + k, D)},
            device_id_type=MESH,
        )
        c.start()
        copies.append(c)
    for c in copies:
        c.wait()
    out_ref[me] = req_ref[me]
    for k in range(1, D):
        out_ref[lax.rem(me - k + D, D)] = land[k]


def gather_kernel(D, cap, half, want_ref, val_ref, *rest):
    outs, sem = rest[:-1], rest[-1]

    def run(h, act):
        def peer(p, carry):
            for s in range(cap):
                w = jnp.maximum(want_ref[p, 0, s], 0)
                act(
                    pltpu.make_async_copy(
                        val_ref.at[w, :, pl.ds(h * half, half)],
                        outs[h].at[p * cap + s],
                        sem.at[h, p * cap + s],
                    )
                )
            return carry

        lax.fori_loop(0, D, peer, 0)

    for h in range(len(outs)):
        run(h, lambda c: c.start())
    for h in range(len(outs)):
        run(h, lambda c: c.wait())


def transposed_dot(tile, right):
    return lax.dot_general(tile, right, (((0,), (0,)), ((), ())), preferred_element_type=jnp.float32)


def continuation(M, first, look_ref, table, tiles):
    weights, values = [], []
    for n in range(M):
        row = look_ref[first + n]
        keep = jnp.where(row >= 0, 1.0, 0.0).astype(jnp.float32)
        tile = tiles(n)
        weights.append(tile * jnp.full(tile.shape, keep, jnp.float32).astype(jnp.bfloat16))
        values.append(table[jnp.maximum(row, 0)])
    return jnp.dot(
        jnp.concatenate(weights, axis=1), jnp.concatenate(values, axis=0), preferred_element_type=jnp.float32
    )


def fetch_value_kernel(G, rows, D, look_ref, from_ref, val_ref, *rest):
    H = (len(rest) - 14) // 2
    outs, rest = rest[:H], rest[H:]
    body, lands = rest[:9], rest[9 : 9 + H - 1]
    acc, table, kept, sem, send, recv = rest[9 + H - 1 :]
    step = pl.program_id(0)
    B, C, V = val_ref.shape[0], outs[0].shape[0], outs[0].shape[2]
    cap = C // D
    me = lax.axis_index("state")

    def copy(h, k):
        to = lax.rem(me + k, D)
        land = table.at[pl.ds(B + me * cap, cap)] if h == 0 else lands[h - 1].at[pl.ds(me * cap, cap)]
        return pltpu.make_async_remote_copy(
            src_ref=outs[h].at[pl.ds(to * cap, cap)],
            dst_ref=land,
            send_sem=send.at[h, k],
            recv_sem=recv.at[h, k],
            device_id={"state": to},
            device_id_type=MESH,
        )

    @pl.when(step == 0)
    def _():
        greet("state", [{"state": lax.rem(me + k, D)} for k in range(1, D)])
        for h in range(H):
            for k in range(1, D):
                copy(h, k).start()
        own = pltpu.make_async_copy(val_ref.at[:, :, pl.ds(0, V)], table.at[pl.ds(0, B)], sem.at[0])
        mine = pltpu.make_async_copy(
            outs[0].at[pl.ds(me * cap, cap)], table.at[pl.ds(B + me * cap, cap)], sem.at[1]
        )
        own.start()
        mine.start()
        own.wait()
        mine.wait()
        for k in range(1, D):
            copy(0, k).wait()

    work(G, rows, look_ref, from_ref, *body, acc, table, kept)

    @pl.when(step == pl.num_programs(0) - 1)
    def _():
        for h in range(1, H):
            for k in range(1, D):
                copy(h, k).wait()


def value_kernel(
    G, rows, col, look_ref, from_ref, val_ref, inc_ref, tiles_ref, cot_ref, util_ref, taste_ref, *rest
):
    before_ref = rest[0]
    value_ref, scaled_ref, out_ref, gu_ref, gt_ref, acc, table, kept, sem = rest[-9:]
    step = pl.program_id(0)
    B, C, V = val_ref.shape[0], inc_ref.shape[0], inc_ref.shape[2]

    @pl.when(step == 0)
    def _():
        own = pltpu.make_async_copy(val_ref.at[:, :, pl.ds(col, V)], table.at[pl.ds(0, B)], sem.at[0])
        far = pltpu.make_async_copy(inc_ref, table.at[pl.ds(B, C)], sem.at[1])
        own.start()
        far.start()
        own.wait()
        far.wait()

    value_ref[:, :col] = before_ref[...]
    work(
        G, rows, look_ref, from_ref, tiles_ref, cot_ref, util_ref, taste_ref,
        value_ref.at[:, col:], scaled_ref, out_ref, gu_ref, gt_ref, acc, table, kept,
    )


def work(
    G, rows, look_ref, from_ref, tiles_ref, cot_ref, util_ref, taste_ref,
    value_ref, scaled_ref, out_ref, gu_ref, gt_ref, acc, table, kept,
):
    step = pl.program_id(0)
    _, A, M, R, _ = tiles_ref.shape
    C = out_ref.shape[0]

    @pl.when(step == 0)
    def _():
        gt_ref[...] = jnp.zeros_like(gt_ref)

    t0, t1 = taste_ref[0:1, :], taste_ref[1:2, :]
    for g in range(G):
        i = step * G + g
        for a in range(A):
            acc[g, a] = continuation(M, (i * A + a) * M, look_ref, table, lambda n: tiles_ref[i, a, n])
    for g in range(G):
        g0 = g1 = 0.0
        for c in range(0, R, rows):
            at = slice(c, c + rows)
            here = slice(g * R + c, g * R + c + rows)
            util = util_ref[g, at, :]
            q0 = util[:, 0:1] + t0 + 0.95 * acc[g, 0, at, :]
            q1 = util[:, 1:2] + t1 + 0.95 * acc[g, 1, at, :]
            gap = q1 - q0
            small = jnp.exp(-jnp.abs(gap))
            total = 1.0 + small
            value_ref[here, :] = jnp.maximum(q0, q1) + jnp.log(total)
            big = cot_ref[here, :].astype(jnp.float32) / total
            little = big * small
            first_wins = gap <= 0.0
            h0 = jnp.where(first_wins, big, little)
            h1 = jnp.where(first_wins, little, big)
            scaled_ref[g, 0, at, :] = (0.95 * h0).astype(jnp.bfloat16)
            scaled_ref[g, 1, at, :] = (0.95 * h1).astype(jnp.bfloat16)
            gu_ref[g, at, 0:1] = jnp.sum(h0, axis=1, keepdims=True)
            gu_ref[g, at, 1:2] = jnp.sum(h1, axis=1, keepdims=True)
            g0, g1 = g0 + h0, g1 + h1
        gt_ref[0:1, :] += jnp.sum(g0, axis=0, keepdims=True)
        gt_ref[1:2, :] += jnp.sum(g1, axis=0, keepdims=True)
    kept[pl.ds(step * G, G)] = scaled_ref[...]

    @pl.when(step == pl.num_programs(0) - 1)
    def _():
        def back(q, carry):
            for u in range(2):
                slot = q * 2 + u
                e = from_ref[slot]
                pair = lax.div(e, M)
                i = lax.div(pair, A)
                a = pair - i * A
                out_ref[slot] = transposed_dot(tiles_ref[i, a, e - pair * M], kept[i, a]).astype(jnp.bfloat16)
            return carry

        lax.fori_loop(0, C // 2, back, 0)


def back_kernel(G, A, M, look_ref, tiles_ref, scaled_ref, adj_ref):
    spare = adj_ref.shape[0] - 1
    step = pl.program_id(0)

    @pl.when(step == 0)
    def _():
        adj_ref[...] = jnp.zeros_like(adj_ref)

    for g in range(G):
        i = step * G + g
        for a in range(A):
            for n in range(M):
                block = look_ref[(i * A + a) * M + n]
                here = jnp.where((block >= 0) & (block < spare), block, spare)
                adj_ref[here] += transposed_dot(tiles_ref[g, a, n], scaled_ref[g, a])


def sums_kernel(D, T, gu_ref, gt_ref, token_ref, after_ref, ou_ref, ot_ref, lu, lt, us, ur, ts, tr):
    ms, mt = lax.axis_index("state"), lax.axis_index("type")
    peers = [{"state": lax.rem(ms + k, D)} for k in range(1, D)]
    peers += [{"type": lax.rem(mt + k, T)} for k in range(1, T)]
    greet("state", peers)
    copies = []
    for k in range(1, T):
        copies.append(
            pltpu.make_async_remote_copy(
                src_ref=gu_ref, dst_ref=lu.at[k], send_sem=us.at[k], recv_sem=ur.at[k],
                device_id={"type": lax.rem(mt + k, T)}, device_id_type=MESH,
            )
        )
    for k in range(1, D):
        copies.append(
            pltpu.make_async_remote_copy(
                src_ref=gt_ref, dst_ref=lt.at[k], send_sem=ts.at[k], recv_sem=tr.at[k],
                device_id={"state": lax.rem(ms + k, D)}, device_id_type=MESH,
            )
        )
    for c in copies:
        c.start()
    for c in copies:
        c.wait()
    lu[0] = gu_ref[...]
    lt[0] = gt_ref[...]
    u = lu[lax.rem(mt, T)]
    for j in range(1, T):
        u = u + lu[lax.rem(mt - j + T, T)]
    t = lt[lax.rem(ms, D)]
    for j in range(1, D):
        t = t + lt[lax.rem(ms - j + D, D)]
    ou_ref[...] = u
    ot_ref[...] = t


def land_kernel(D, cap, want_ref, adj_ref, ret_ref, *rest):
    out_ref, done_ref = rest[-2:]
    done_ref[0] = 0
    out_ref[...] = adj_ref[...]

    def peer(p, carry):
        for s in range(cap):
            w = want_ref[p, 0, s]

            @pl.when(w >= 0)
            def _():
                out_ref[w] += ret_ref[p * cap + s].astype(jnp.float32)

        return carry

    lax.fori_loop(0, D, peer, 0)


def local(value_in, cotangent, state_util, taste, tiles, dest_block, counts):
    B, A, M, R, _ = tiles.shape
    W = value_in.shape[1]
    D = lax.axis_size("state")
    T = lax.axis_size("type")
    cap = max(2, (B + D - 2) // (D - 1))
    E, C = B * A * M, D * cap
    f32, bf16, i32 = jnp.float32, jnp.bfloat16, jnp.int32
    shape = jax.ShapeDtypeStruct
    values = value_in.reshape(B, R, W)

    req, look, origin = pl.pallas_call(
        functools.partial(plan_kernel, (B, A, M, D, cap)),
        out_shape=(shape((D, 1, 128), i32), shape((E,), i32), shape((C,), i32)),
        in_specs=[smem()] * 3,
        out_specs=[smem()] * 3,
        scratch_shapes=[SMEM((D,), i32)],
        name="plan",
    )(lax.axis_index("state").reshape(1).astype(i32), dest_block.transpose(2, 1, 0), counts.T)

    wanted = pl.pallas_call(
        functools.partial(request_kernel, D),
        out_shape=shape((D, 1, 128), i32),
        in_specs=[pl.BlockSpec(memory_space=VMEM)],
        out_specs=pl.BlockSpec(memory_space=VMEM),
        scratch_shapes=[VMEM((D, 1, 128), i32), pltpu.SemaphoreType.DMA((D,)), pltpu.SemaphoreType.DMA((D,))],
        compiler_params=pltpu.CompilerParams(collective_id=0, has_side_effects=True),
        name="request",
    )(req)

    H = 2 if W % 256 == 0 else 1
    V = W // H
    G = 4 if B % 4 == 0 else 1
    outgoing = pl.pallas_call(
        functools.partial(gather_kernel, D, cap, V),
        out_shape=tuple(shape((C, R, V), bf16) for h in range(H)),
        in_specs=[smem(), pl.BlockSpec(memory_space=VMEM)],
        out_specs=[pl.BlockSpec(memory_space=pl.ANY)] * H,
        scratch_shapes=[pltpu.SemaphoreType.DMA((H, C))],
        name="gather",
    )(wanted, values)

    def exchange(x):
        return lax.all_to_all(
            x.reshape(D, cap, R, V), "state", split_axis=0, concat_axis=0, tiled=True
        ).reshape(C, R, V)

    incoming = []

    flops = 2 * E * R * R * W
    util_cols = state_util.reshape(A, B, R).transpose(1, 2, 0)
    value = None
    gus, gts, outbound, scaleds = [], [], [], []
    any_spec = pl.BlockSpec(memory_space=pl.ANY)
    for h in range(H):
        wide = V * (h + 1)
        ins = [
            whole((B, A, M, R, R)),
            pl.BlockSpec((G * R, V), lambda i, h=h: (i, h)),
            pl.BlockSpec((G, R, A), lambda i: (i, 0, 0)),
            pl.BlockSpec((A, V), lambda i, h=h: (0, h)),
        ]
        out_shape = [
            shape((B * R, wide), f32), shape((B, A, R, V), bf16), shape((C, R, V), bf16),
            shape((B, R, A), f32), shape((A, V), f32),
        ]
        out_specs = [
            pl.BlockSpec((G * R, wide), lambda i: (i, 0)),
            pl.BlockSpec((G, A, R, V), lambda i: (i, 0, 0, 0)),
            whole((C, R, V)),
            pl.BlockSpec((G, R, A), lambda i: (i, 0, 0)),
            whole((A, V)),
        ]
        scratch = [
            VMEM((G, A, R, V), f32), VMEM((B + C, R, V), bf16), VMEM((B, A, R, V), bf16),
            pltpu.SemaphoreType.DMA((2,)),
        ]
        cost = pl.CostEstimate(flops=flops // H, bytes_accessed=(24 << 20) // H, transcendentals=3 * B * R * V)
        if h == 0:
            value, scaled, out, gu, gt, *incoming = pl.pallas_call(
                functools.partial(fetch_value_kernel, G, 32, D),
                grid=(B // G,),
                out_shape=out_shape + [shape((C, R, V), bf16)] * (H - 1),
                in_specs=[smem(), smem(), any_spec] + [any_spec] * H + ins,
                out_specs=out_specs + [any_spec] * (H - 1),
                scratch_shapes=scratch + [pltpu.SemaphoreType.DMA((H, D)), pltpu.SemaphoreType.DMA((H, D))],
                compiler_params=pltpu.CompilerParams(collective_id=2, has_side_effects=True),
                cost_estimate=cost,
                name="fetch",
            )(look, origin, values, *outgoing, tiles, cotangent, util_cols, taste)
        else:
            value, scaled, out, gu, gt = pl.pallas_call(
                functools.partial(value_kernel, G, 32, h * V),
                grid=(B // G,),
                out_shape=out_shape,
                in_specs=[smem(), smem(), any_spec, any_spec] + ins
                + [pl.BlockSpec((G * R, h * V), lambda i: (i, 0))],
                out_specs=out_specs,
                scratch_shapes=scratch,
                cost_estimate=cost,
                name="value",
            )(look, origin, values, incoming[h - 1], tiles, cotangent, util_cols, taste, value)
        outbound.append(out)
        scaleds.append(scaled)
        gus.append(gu)
        gts.append(gt)

    adjs = [
        pl.pallas_call(
            functools.partial(back_kernel, G, A, M),
            grid=(B // G,),
            out_shape=shape((B + 1, R, V), f32),
            in_specs=[
                smem(),
                pl.BlockSpec((G, A, M, R, R), lambda i: (i, 0, 0, 0, 0)),
                pl.BlockSpec((G, A, R, V), lambda i: (i, 0, 0, 0)),
            ],
            out_specs=whole((B + 1, R, V)),
            cost_estimate=pl.CostEstimate(flops=flops // H, bytes_accessed=(14 << 20) // H, transcendentals=0),
            name="back",
        )(look, tiles, x)
        for x in scaleds
    ]

    returned = []
    for h in range(H):
        if h > 0:
            outbound[h], adjs[h - 1] = lax.optimization_barrier((outbound[h], adjs[h - 1]))
        returned.append(exchange(outbound[h]))

    adjoint, tokens = None, []
    gu_rows = sum(gus).transpose(2, 0, 1).reshape(A, B * R) / (W * T)
    for h in range(H):
        held = [] if h == 0 else [adjoint]
        adjoint, token = pl.pallas_call(
            functools.partial(land_kernel, D, cap),
            grid=(1,),
            out_shape=(shape((B, R, W), f32), shape((1,), i32)),
            in_specs=[smem(), whole((B, R, V)), whole((C, R, V))]
            + [pl.BlockSpec(memory_space=pl.ANY)] * len(held),
            out_specs=[pl.BlockSpec((B, R, V), lambda j, h=h: (0, 0, h)), smem()],
            input_output_aliases={3 + k: k for k in range(len(held))},
            name="land",
        )(wanted, adjs[h], returned[h], *held)
        tokens.append(token)
    grad_util, grad_taste = pl.pallas_call(
        functools.partial(sums_kernel, D, T),
        out_shape=(shape((A, B * R), f32), shape((A, W), f32)),
        in_specs=[pl.BlockSpec(memory_space=VMEM)] * 2 + [smem(), pl.BlockSpec(memory_space=pl.ANY)],
        out_specs=[pl.BlockSpec(memory_space=VMEM)] * 2,
        scratch_shapes=[
            VMEM((T, A, B * R), f32), VMEM((D, A, W), f32),
            pltpu.SemaphoreType.DMA((T,)), pltpu.SemaphoreType.DMA((T,)),
            pltpu.SemaphoreType.DMA((D,)), pltpu.SemaphoreType.DMA((D,)),
        ],
        compiler_params=pltpu.CompilerParams(collective_id=1, has_side_effects=True),
        cost_estimate=pl.CostEstimate(flops=0, bytes_accessed=8 << 20, transcendentals=0),
        name="sums",
    )(gu_rows, jnp.concatenate(gts, axis=1) / (B * R * D), tokens[0], adjs[-1])

    return value, adjoint.reshape(B * R, W), grad_util, grad_taste


def solution(mesh):
    rows = ("groups", "state")
    return jax.shard_map(
        local,
        mesh=mesh,
        in_specs=(
            P(rows, "type"),
            P(rows, "type"),
            P(None, rows),
            P(None, ("groups", "type")),
            P(rows, None, None, None, None),
            P(rows, None, None),
            P(rows, None),
        ),
        out_specs=(P(rows, "type"), P(rows, "type"), P(None, rows), P(None, ("groups", "type"))),
        check_vma=False,
    )
```

```python
import functools

import jax
import jax.numpy as jnp
from jax import lax
from jax.experimental import pallas as pl
from jax.experimental.pallas import tpu as pltpu
from jax.sharding import PartitionSpec as P

VMEM = pltpu.VMEM
SMEM = pltpu.SMEM
MESH = pl.DeviceIdType.MESH


def smem():
    return pl.BlockSpec(memory_space=SMEM)


def whole(shape):
    return pl.BlockSpec(shape, lambda *g: (0,) * len(shape))


def plan_kernel(dims, me_ref, dest_ref, count_ref, req_ref, look_ref, from_ref, fill):
    B, A, M, D, cap = dims
    me = me_ref[0]

    def clear(p, carry):
        fill[p] = 0
        for s in range(cap):
            req_ref[p, 0, s] = -1
            from_ref[p * cap + s] = 0
        return carry

    lax.fori_loop(0, D, clear, 0)

    def lists(i, carry):
        for a in range(A):
            count = count_ref[a, i]
            for n in range(M):
                e = (i * A + a) * M + n
                dest = dest_ref[n, a, i]
                owner = lax.div(dest, B)
                block = dest - owner * B
                used = n < count
                look_ref[e] = jnp.where(used & (owner == me), block, -1)

                @pl.when(used & (owner != me))
                def _():
                    s = fill[owner]
                    fill[owner] = s + 1
                    req_ref[owner, 0, s] = block
                    from_ref[owner * cap + s] = e
                    look_ref[e] = B + owner * cap + s

        return carry

    lax.fori_loop(0, B, lists, 0)


def greet(axis, others):
    barrier = pltpu.get_barrier_semaphore()
    for ids in others:
        pl.semaphore_signal(barrier, inc=1, device_id=ids, device_id_type=MESH)
    pl.semaphore_wait(barrier, len(others))


def request_kernel(D, req_ref, out_ref, land, send, recv):
    me = lax.axis_index("state")
    peers = [{"state": lax.rem(me + k, D)} for k in range(1, D)]
    greet("state", peers)
    copies = []
    for k in range(1, D):
        c = pltpu.make_async_remote_copy(
            src_ref=req_ref.at[lax.rem(me + k, D)],
            dst_ref=land.at[k],
            send_sem=send.at[k],
            recv_sem=recv.at[k],
            device_id={"state": lax.rem(me + k, D)},
            device_id_type=MESH,
        )
        c.start()
        copies.append(c)
    for c in copies:
        c.wait()
    out_ref[me] = req_ref[me]
    for k in range(1, D):
        out_ref[lax.rem(me - k + D, D)] = land[k]


def gather_kernel(D, cap, half, want_ref, val_ref, *rest):
    outs, sem = rest[:-1], rest[-1]

    def run(h, act):
        def peer(p, carry):
            for s in range(cap):
                w = jnp.maximum(want_ref[p, 0, s], 0)
                act(
                    pltpu.make_async_copy(
                        val_ref.at[w, :, pl.ds(h * half, half)],
                        outs[h].at[p * cap + s],
                        sem.at[h, p * cap + s],
                    )
                )
            return carry

        lax.fori_loop(0, D, peer, 0)

    for h in range(len(outs)):
        run(h, lambda c: c.start())
    for h in range(len(outs)):
        run(h, lambda c: c.wait())


def transposed_dot(tile, right):
    return lax.dot_general(tile, right, (((0,), (0,)), ((), ())), preferred_element_type=jnp.float32)


def continuation(M, first, look_ref, table, tiles):
    weights, values = [], []
    for n in range(M):
        row = look_ref[first + n]
        keep = jnp.where(row >= 0, 1.0, 0.0).astype(jnp.float32)
        tile = tiles(n)
        weights.append(tile * jnp.full(tile.shape, keep, jnp.float32).astype(jnp.bfloat16))
        values.append(table[jnp.maximum(row, 0)])
    return jnp.dot(
        jnp.concatenate(weights, axis=1), jnp.concatenate(values, axis=0), preferred_element_type=jnp.float32
    )


def fetch_value_kernel(G, rows, D, look_ref, from_ref, val_ref, *rest):
    H = (len(rest) - 14) // 2
    outs, rest = rest[:H], rest[H:]
    body, lands = rest[:9], rest[9 : 9 + H - 1]
    acc, table, kept, sem, send, recv = rest[9 + H - 1 :]
    step = pl.program_id(0)
    B, C, V = val_ref.shape[0], outs[0].shape[0], outs[0].shape[2]
    cap = C // D
    me = lax.axis_index("state")

    def copy(h, k):
        to = lax.rem(me + k, D)
        land = table.at[pl.ds(B + me * cap, cap)] if h == 0 else lands[h - 1].at[pl.ds(me * cap, cap)]
        return pltpu.make_async_remote_copy(
            src_ref=outs[h].at[pl.ds(to * cap, cap)],
            dst_ref=land,
            send_sem=send.at[h, k],
            recv_sem=recv.at[h, k],
            device_id={"state": to},
            device_id_type=MESH,
        )

    @pl.when(step == 0)
    def _():
        greet("state", [{"state": lax.rem(me + k, D)} for k in range(1, D)])
        for h in range(H):
            for k in range(1, D):
                copy(h, k).start()
        own = pltpu.make_async_copy(val_ref.at[:, :, pl.ds(0, V)], table.at[pl.ds(0, B)], sem.at[0])
        mine = pltpu.make_async_copy(
            outs[0].at[pl.ds(me * cap, cap)], table.at[pl.ds(B + me * cap, cap)], sem.at[1]
        )
        own.start()
        mine.start()
        own.wait()
        mine.wait()
        for k in range(1, D):
            copy(0, k).wait()

    work(G, rows, look_ref, from_ref, *body, acc, table, kept)

    @pl.when(step == pl.num_programs(0) - 1)
    def _():
        for h in range(1, H):
            for k in range(1, D):
                copy(h, k).wait()


def value_kernel(
    G, rows, col, look_ref, from_ref, val_ref, inc_ref, tiles_ref, cot_ref, util_ref, taste_ref, *rest
):
    before_ref = rest[0]
    value_ref, scaled_ref, out_ref, gu_ref, gt_ref, acc, table, kept, sem = rest[-9:]
    step = pl.program_id(0)
    B, C, V = val_ref.shape[0], inc_ref.shape[0], inc_ref.shape[2]

    @pl.when(step == 0)
    def _():
        own = pltpu.make_async_copy(val_ref.at[:, :, pl.ds(col, V)], table.at[pl.ds(0, B)], sem.at[0])
        far = pltpu.make_async_copy(inc_ref, table.at[pl.ds(B, C)], sem.at[1])
        own.start()
        far.start()
        own.wait()
        far.wait()

    value_ref[:, :col] = before_ref[...]
    work(
        G, rows, look_ref, from_ref, tiles_ref, cot_ref, util_ref, taste_ref,
        value_ref.at[:, col:], scaled_ref, out_ref, gu_ref, gt_ref, acc, table, kept,
    )


def work(
    G, rows, look_ref, from_ref, tiles_ref, cot_ref, util_ref, taste_ref,
    value_ref, scaled_ref, out_ref, gu_ref, gt_ref, acc, table, kept,
):
    step = pl.program_id(0)
    _, A, M, R, _ = tiles_ref.shape
    C = out_ref.shape[0]

    @pl.when(step == 0)
    def _():
        gt_ref[...] = jnp.zeros_like(gt_ref)

    t0, t1 = taste_ref[0:1, :], taste_ref[1:2, :]
    for g in range(G):
        i = step * G + g
        for a in range(A):
            acc[g, a] = continuation(M, (i * A + a) * M, look_ref, table, lambda n: tiles_ref[i, a, n])
    for g in range(G):
        g0 = g1 = 0.0
        cols = [
            jnp.transpose(jnp.broadcast_to(util_ref[a : a + 1, g * R : (g + 1) * R], (R, R))) for a in range(A)
        ]
        for c in range(0, R, rows):
            at = slice(c, c + rows)
            here = slice(g * R + c, g * R + c + rows)
            q0 = cols[0][at, 0:1] + t0 + 0.95 * acc[g, 0, at, :]
            q1 = cols[1][at, 0:1] + t1 + 0.95 * acc[g, 1, at, :]
            gap = q1 - q0
            small = jnp.exp(-jnp.abs(gap))
            total = 1.0 + small
            value_ref[here, :] = jnp.maximum(q0, q1) + jnp.log(total)
            big = cot_ref[here, :].astype(jnp.float32) / total
            little = big * small
            first_wins = gap <= 0.0
            h0 = jnp.where(first_wins, big, little)
            h1 = jnp.where(first_wins, little, big)
            scaled_ref[g, 0, at, :] = (0.95 * h0).astype(jnp.bfloat16)
            scaled_ref[g, 1, at, :] = (0.95 * h1).astype(jnp.bfloat16)
            gu_ref[g, at, 0:1] = jnp.sum(h0, axis=1, keepdims=True)
            gu_ref[g, at, 1:2] = jnp.sum(h1, axis=1, keepdims=True)
            g0, g1 = g0 + h0, g1 + h1
        gt_ref[0:1, :] += jnp.sum(g0, axis=0, keepdims=True)
        gt_ref[1:2, :] += jnp.sum(g1, axis=0, keepdims=True)
    kept[pl.ds(step * G, G)] = scaled_ref[...]

    @pl.when(step == pl.num_programs(0) - 1)
    def _():
        def back(q, carry):
            for u in range(2):
                slot = q * 2 + u
                e = from_ref[slot]
                pair = lax.div(e, M)
                i = lax.div(pair, A)
                a = pair - i * A
                out_ref[slot] = transposed_dot(tiles_ref[i, a, e - pair * M], kept[i, a]).astype(jnp.bfloat16)
            return carry

        lax.fori_loop(0, C // 2, back, 0)


def back_kernel(G, A, M, look_ref, tiles_ref, scaled_ref, adj_ref):
    spare = adj_ref.shape[0] - 1
    step = pl.program_id(0)

    @pl.when(step == 0)
    def _():
        adj_ref[...] = jnp.zeros_like(adj_ref)

    for g in range(G):
        i = step * G + g
        for a in range(A):
            for n in range(M):
                block = look_ref[(i * A + a) * M + n]
                here = jnp.where((block >= 0) & (block < spare), block, spare)
                adj_ref[here] += transposed_dot(tiles_ref[g, a, n], scaled_ref[g, a])


def sums_kernel(D, T, gu_ref, gt_ref, token_ref, after_ref, ou_ref, ot_ref, lu, lt, us, ur, ts, tr):
    ms, mt = lax.axis_index("state"), lax.axis_index("type")
    peers = [{"state": lax.rem(ms + k, D)} for k in range(1, D)]
    peers += [{"type": lax.rem(mt + k, T)} for k in range(1, T)]
    greet("state", peers)
    copies = []
    for k in range(1, T):
        copies.append(
            pltpu.make_async_remote_copy(
                src_ref=gu_ref, dst_ref=lu.at[k], send_sem=us.at[k], recv_sem=ur.at[k],
                device_id={"type": lax.rem(mt + k, T)}, device_id_type=MESH,
            )
        )
    for k in range(1, D):
        copies.append(
            pltpu.make_async_remote_copy(
                src_ref=gt_ref, dst_ref=lt.at[k], send_sem=ts.at[k], recv_sem=tr.at[k],
                device_id={"state": lax.rem(ms + k, D)}, device_id_type=MESH,
            )
        )
    for c in copies:
        c.start()
    for c in copies:
        c.wait()
    lu[0] = gu_ref[...]
    lt[0] = gt_ref[...]
    u = lu[lax.rem(mt, T)]
    for j in range(1, T):
        u = u + lu[lax.rem(mt - j + T, T)]
    t = lt[lax.rem(ms, D)]
    for j in range(1, D):
        t = t + lt[lax.rem(ms - j + D, D)]
    ou_ref[...] = u
    ot_ref[...] = t


def land_kernel(D, cap, want_ref, adj_ref, ret_ref, *rest):
    out_ref, done_ref = rest[-2:]
    done_ref[0] = 0
    out_ref[...] = adj_ref[...]

    def peer(p, carry):
        for s in range(cap):
            w = want_ref[p, 0, s]

            @pl.when(w >= 0)
            def _():
                out_ref[w] += ret_ref[p * cap + s].astype(jnp.float32)

        return carry

    lax.fori_loop(0, D, peer, 0)


def local(value_in, cotangent, state_util, taste, tiles, dest_block, counts):
    B, A, M, R, _ = tiles.shape
    W = value_in.shape[1]
    D = lax.axis_size("state")
    T = lax.axis_size("type")
    cap = max(2, (B + D - 2) // (D - 1))
    E, C = B * A * M, D * cap
    f32, bf16, i32 = jnp.float32, jnp.bfloat16, jnp.int32
    shape = jax.ShapeDtypeStruct
    values = value_in.reshape(B, R, W)

    req, look, origin = pl.pallas_call(
        functools.partial(plan_kernel, (B, A, M, D, cap)),
        out_shape=(shape((D, 1, 128), i32), shape((E,), i32), shape((C,), i32)),
        in_specs=[smem()] * 3,
        out_specs=[smem()] * 3,
        scratch_shapes=[SMEM((D,), i32)],
        name="plan",
    )(lax.axis_index("state").reshape(1).astype(i32), dest_block.transpose(2, 1, 0), counts.T)

    wanted = pl.pallas_call(
        functools.partial(request_kernel, D),
        out_shape=shape((D, 1, 128), i32),
        in_specs=[pl.BlockSpec(memory_space=VMEM)],
        out_specs=pl.BlockSpec(memory_space=VMEM),
        scratch_shapes=[VMEM((D, 1, 128), i32), pltpu.SemaphoreType.DMA((D,)), pltpu.SemaphoreType.DMA((D,))],
        compiler_params=pltpu.CompilerParams(collective_id=0, has_side_effects=True),
        name="request",
    )(req)

    H = 2 if W % 256 == 0 else 1
    V = W // H
    G = 4 if B % 4 == 0 else 1
    outgoing = pl.pallas_call(
        functools.partial(gather_kernel, D, cap, V),
        out_shape=tuple(shape((C, R, V), bf16) for h in range(H)),
        in_specs=[smem(), pl.BlockSpec(memory_space=VMEM)],
        out_specs=[pl.BlockSpec(memory_space=pl.ANY)] * H,
        scratch_shapes=[pltpu.SemaphoreType.DMA((H, C))],
        name="gather",
    )(wanted, values)

    def exchange(x):
        return lax.all_to_all(
            x.reshape(D, cap, R, V), "state", split_axis=0, concat_axis=0, tiled=True
        ).reshape(C, R, V)

    incoming = []

    flops = 2 * E * R * R * W
    value = None
    gus, gts, outbound, scaleds = [], [], [], []
    any_spec = pl.BlockSpec(memory_space=pl.ANY)
    for h in range(H):
        wide = V * (h + 1)
        ins = [
            whole((B, A, M, R, R)),
            pl.BlockSpec((G * R, V), lambda i, h=h: (i, h)),
            pl.BlockSpec((A, G * R), lambda i: (0, i)),
            pl.BlockSpec((A, V), lambda i, h=h: (0, h)),
        ]
        out_shape = [
            shape((B * R, wide), f32), shape((B, A, R, V), bf16), shape((C, R, V), bf16),
            shape((B, R, A), f32), shape((A, V), f32),
        ]
        out_specs = [
            pl.BlockSpec((G * R, wide), lambda i: (i, 0)),
            pl.BlockSpec((G, A, R, V), lambda i: (i, 0, 0, 0)),
            whole((C, R, V)),
            pl.BlockSpec((G, R, A), lambda i: (i, 0, 0)),
            whole((A, V)),
        ]
        scratch = [
            VMEM((G, A, R, V), f32), VMEM((B + C, R, V), bf16), VMEM((B, A, R, V), bf16),
            pltpu.SemaphoreType.DMA((2,)),
        ]
        cost = pl.CostEstimate(flops=flops // H, bytes_accessed=(24 << 20) // H, transcendentals=3 * B * R * V)
        if h == 0:
            value, scaled, out, gu, gt, *incoming = pl.pallas_call(
                functools.partial(fetch_value_kernel, G, 32, D),
                grid=(B // G,),
                out_shape=out_shape + [shape((C, R, V), bf16)] * (H - 1),
                in_specs=[smem(), smem(), any_spec] + [any_spec] * H + ins,
                out_specs=out_specs + [any_spec] * (H - 1),
                scratch_shapes=scratch + [pltpu.SemaphoreType.DMA((H, D)), pltpu.SemaphoreType.DMA((H, D))],
                compiler_params=pltpu.CompilerParams(collective_id=2, has_side_effects=True),
                cost_estimate=cost,
                name="fetch",
            )(look, origin, values, *outgoing, tiles, cotangent, state_util, taste)
        else:
            value, scaled, out, gu, gt = pl.pallas_call(
                functools.partial(value_kernel, G, 32, h * V),
                grid=(B // G,),
                out_shape=out_shape,
                in_specs=[smem(), smem(), any_spec, any_spec] + ins
                + [pl.BlockSpec((G * R, h * V), lambda i: (i, 0))],
                out_specs=out_specs,
                scratch_shapes=scratch,
                cost_estimate=cost,
                name="value",
            )(look, origin, values, incoming[h - 1], tiles, cotangent, state_util, taste, value)
        outbound.append(out)
        scaleds.append(scaled)
        gus.append(gu)
        gts.append(gt)

    adjs = [
        pl.pallas_call(
            functools.partial(back_kernel, G, A, M),
            grid=(B // G,),
            out_shape=shape((B + 1, R, V), f32),
            in_specs=[
                smem(),
                pl.BlockSpec((G, A, M, R, R), lambda i: (i, 0, 0, 0, 0)),
                pl.BlockSpec((G, A, R, V), lambda i: (i, 0, 0, 0)),
            ],
            out_specs=whole((B + 1, R, V)),
            cost_estimate=pl.CostEstimate(flops=flops // H, bytes_accessed=(14 << 20) // H, transcendentals=0),
            name="back",
        )(look, tiles, x)
        for x in scaleds
    ]

    returned = []
    for h in range(H):
        if h > 0:
            outbound[h], adjs[h - 1] = lax.optimization_barrier((outbound[h], adjs[h - 1]))
        returned.append(exchange(outbound[h]))

    adjoint, tokens = None, []
    gu_rows = sum(gus).transpose(2, 0, 1).reshape(A, B * R) / (W * T)
    for h in range(H):
        held = [] if h == 0 else [adjoint]
        adjoint, token = pl.pallas_call(
            functools.partial(land_kernel, D, cap),
            grid=(1,),
            out_shape=(shape((B, R, W), f32), shape((1,), i32)),
            in_specs=[smem(), whole((B, R, V)), whole((C, R, V))]
            + [pl.BlockSpec(memory_space=pl.ANY)] * len(held),
            out_specs=[pl.BlockSpec((B, R, V), lambda j, h=h: (0, 0, h)), smem()],
            input_output_aliases={3 + k: k for k in range(len(held))},
            name="land",
        )(wanted, adjs[h], returned[h], *held)
        tokens.append(token)
    grad_util, grad_taste = pl.pallas_call(
        functools.partial(sums_kernel, D, T),
        out_shape=(shape((A, B * R), f32), shape((A, W), f32)),
        in_specs=[pl.BlockSpec(memory_space=VMEM)] * 2 + [smem(), pl.BlockSpec(memory_space=pl.ANY)],
        out_specs=[pl.BlockSpec(memory_space=VMEM)] * 2,
        scratch_shapes=[
            VMEM((T, A, B * R), f32), VMEM((D, A, W), f32),
            pltpu.SemaphoreType.DMA((T,)), pltpu.SemaphoreType.DMA((T,)),
            pltpu.SemaphoreType.DMA((D,)), pltpu.SemaphoreType.DMA((D,)),
        ],
        compiler_params=pltpu.CompilerParams(collective_id=1, has_side_effects=True),
        cost_estimate=pl.CostEstimate(flops=0, bytes_accessed=8 << 20, transcendentals=0),
        name="sums",
    )(gu_rows, jnp.concatenate(gts, axis=1) / (B * R * D), tokens[0], adjs[-1])

    return value, adjoint.reshape(B * R, W), grad_util, grad_taste


def solution(mesh):
    rows = ("groups", "state")
    return jax.shard_map(
        local,
        mesh=mesh,
        in_specs=(
            P(rows, "type"),
            P(rows, "type"),
            P(None, rows),
            P(None, ("groups", "type")),
            P(rows, None, None, None, None),
            P(rows, None, None),
            P(rows, None),
        ),
        out_specs=(P(rows, "type"), P(rows, "type"), P(None, rows), P(None, ("groups", "type"))),
        check_vma=False,
    )
```
